1024 devices in a mesh: section: 4 (over x), seq: 128 (over z, y_lo, core), rep: 2 (over y_hi).
Axes of the slice: x: 4, y: 4 (y_hi: 2, y_lo: 2; y = y_hi * 2 + y_lo), z: 32, core: 2. Of those that a mesh axis runs over, the one named last changes fastest.
Arguments:
- signal: bfloat16 [2, 1024, 4, 4096], P(None, 'seq', None, 'rep'), may hold values from -200 to 200, as said below
- head_proj: bfloat16 [4, 32, 128, 384], P('section', 'rep'), may hold values from -2 to 6, as said below
- record_start: int32 [2, 4], replicated, may hold values from 0 to 255
- record_pad: int32 [2, 4], replicated, may hold values from 0 to 255
Outputs:
- layer_out: bfloat16 [4, 2, 1024, 4, 4096], P('section', None, 'seq', None, 'rep')
The draws below stay inside these ranges and needn't reach their ends.
Inputs may be any that keep to these rules, and one draw needn't show every extreme that they name: `signal`: finite. `head_proj`: finite.
All inputs are finite; a program needn't handle non-finite values.
Results may differ from the reference program's by a relative error of at most 0.015.
The reference program's roundings to bfloat16 on the way count: a program that leaves them out, or rounds other values in their place, can miss the bound.
Values may be sent and summed in bfloat16 or wider, within the bound.
A program may use at most 32 MiB of HBM per device.

```python
import math
import jax
import jax.numpy as jnp
from jax import lax

HEADS = 32
HEAD = 128
MB = 2
STATIONS = 4
WIN = 4
TIMES = 1024
LAYERS = 4


def draw_signal(key, part):
    streams = jax.random.split(jax.random.fold_in(key, 11), 4)
    shape_heads = (MB, TIMES, STATIONS, HEADS, HEAD)
    base_draw = jnp.clip(jax.random.normal(streams[0], shape_heads, jnp.float32), -6.0, 6.0)
    row_scale = jnp.exp(jax.random.uniform(streams[1], (MB, TIMES, STATIONS, 1, 1), jnp.float32, math.log(0.03), math.log(0.3)))
    slope = jax.random.uniform(streams[2], (MB, TIMES, STATIONS, 1, 1), jnp.float32, -math.log(16.0), math.log(16.0))
    position = (jnp.arange(HEADS, dtype=jnp.float32) + 0.5) / HEADS - 0.5
    tilt = jnp.exp(slope * position[None, None, None, :, None])
    head_scale = jnp.exp(jax.random.uniform(streams[3], (MB, TIMES, STATIONS, HEADS, 1), jnp.float32, 0.0, math.log(3.0)))
    shaped = base_draw * row_scale * tilt * head_scale
    return shaped.reshape(MB, TIMES, STATIONS, HEADS * HEAD).astype(jnp.bfloat16)


def draw_head_proj(key, part):
    streams = jax.random.split(jax.random.fold_in(key, 23), 3)
    base_draw = jnp.clip(jax.random.normal(streams[0], (LAYERS, HEADS, HEAD, 3 * HEAD), jnp.float32), -6.0, 6.0) / math.sqrt(HEAD)
    value_gain = jnp.exp(jax.random.uniform(streams[2], (LAYERS, HEADS, 1, 1), jnp.float32, -math.log(3.0), math.log(3.0)))
    is_value = (jnp.arange(3 * HEAD) >= 2 * HEAD)[None, None, None, :]
    column_gain = jnp.where(is_value, value_gain, 1.0)
    scaled = base_draw * column_gain
    return scaled.astype(jnp.bfloat16)


def touch_ends(array, stream_key, smallest, top_value):
    longest = array.shape.index(max(array.shape))
    spots = []
    for shift in (0, 1):
        where = [jax.random.randint(jax.random.fold_in(stream_key, axis), (), 0, length) for axis, length in enumerate(array.shape)]
        where[longest] = (where[longest] + shift) % array.shape[longest]
        spots.append(tuple(where))
    return array.at[spots[0]].set(smallest).at[spots[1]].set(top_value)


def setup_inputs(seed: int = 0) -> dict:
    key_of = jax.random.split(jax.random.key(seed), 5)
    return {
        "signal": draw_signal(jax.random.fold_in(key_of[4], 71), 0),
        "head_proj": draw_head_proj(jax.random.fold_in(key_of[4], 71), 0),
        "record_start": touch_ends(jax.random.randint(key_of[2], (MB, STATIONS), 0, TIMES // 4), jax.random.fold_in(key_of[2], 1), 0, (TIMES // 4) - 1).astype(jnp.int32),
        "record_pad": touch_ends(jax.random.randint(key_of[3], (MB, STATIONS), 0, TIMES // 4), jax.random.fold_in(key_of[3], 1), 0, (TIMES // 4) - 1).astype(jnp.int32),
    }


def masked_softmax(scores, allowed):
    scores = jnp.where(allowed, scores, -1e+30)
    row_top = lax.optimization_barrier(jnp.max(scores, axis=-1, keepdims=True))
    weights = jnp.where(allowed, jnp.exp(scores - row_top), 0.0)
    return (weights / lax.optimization_barrier(jnp.sum(weights, axis=-1, keepdims=True))).astype(jnp.bfloat16)

def one_layer(hidden, weights, first_step, pad_steps):
    widened = hidden.astype(jnp.float32)
    squares = lax.optimization_barrier(jnp.sum(widened * widened, axis=-1, keepdims=True))
    normed = (widened * lax.rsqrt(squares / (HEADS * HEAD) + 1e-06)).astype(jnp.bfloat16)
    heads_split = normed.reshape(TIMES, STATIONS, HEADS, HEAD).astype(jnp.float32)
    projected = jnp.einsum('tshd,hde->tshe', heads_split, weights.astype(jnp.float32)).astype(jnp.bfloat16)
    time_steps = jnp.arange(TIMES, dtype=jnp.int32)
    is_valid = (time_steps[None, :] >= first_step[:, None]) & (time_steps[None, :] < TIMES - pad_steps[:, None])
    blocks = TIMES // WIN
    offset = jnp.arange(3 * WIN)[None, :] - jnp.arange(WIN)[:, None]
    in_band = (offset >= 0) & (offset <= 2 * WIN)
    centre = offset == WIN
    padded_valid = jnp.pad(is_valid, ((0, 0), (WIN, WIN))).reshape(STATIONS, blocks + 2, WIN).transpose(1, 0, 2)
    key_valid = jnp.concatenate([padded_valid[:-2], padded_valid[1:-1], padded_valid[2:]], axis=2)
    time_allowed = in_band[None, None] & key_valid[:, :, None, :] | centre[None, None]
    station_allowed = is_valid.T[:, None, :] | jnp.eye(STATIONS, dtype=bool)[None]

    def per_head(per_column):
        queries = per_column[..., :HEAD]
        key_rows = per_column[..., HEAD:2 * HEAD]
        value_rows = per_column[..., 2 * HEAD:]
        key_pad = jnp.pad(key_rows, ((WIN, WIN), (0, 0), (0, 0))).reshape(blocks + 2, WIN, STATIONS, HEAD)
        value_pad = jnp.pad(value_rows, ((WIN, WIN), (0, 0), (0, 0))).reshape(blocks + 2, WIN, STATIONS, HEAD)
        key_blocks = jnp.concatenate([key_pad[:-2], key_pad[1:-1], key_pad[2:]], axis=1)
        value_blocks = jnp.concatenate([value_pad[:-2], value_pad[1:-1], value_pad[2:]], axis=1)
        query_blocks = queries.reshape(blocks, WIN, STATIONS, HEAD)
        scores = jnp.einsum('nasd,nbsd->nsab', query_blocks.astype(jnp.float32), key_blocks.astype(jnp.float32)) / math.sqrt(HEAD)
        time_weights = masked_softmax(scores, time_allowed)
        along_time = jnp.einsum('nsab,nbsd->nasd', time_weights.astype(jnp.float32), value_blocks.astype(jnp.float32)).reshape(TIMES, STATIONS, HEAD)
        station_scores = jnp.einsum('tsd,tzd->tsz', queries.astype(jnp.float32), key_rows.astype(jnp.float32)) / math.sqrt(HEAD)
        station_weights = masked_softmax(station_scores, station_allowed)
        across = jnp.einsum('tsz,tzd->tsd', station_weights.astype(jnp.float32), value_rows.astype(jnp.float32))
        return along_time + across
    head_outs = lax.map(per_head, projected.transpose(2, 0, 1, 3))
    updates = head_outs.transpose(1, 2, 0, 3).reshape(TIMES, STATIONS, HEADS * HEAD)
    return (widened + updates).astype(jnp.bfloat16)

def reference(signal, head_proj, record_start, record_pad):
    results = []
    for micro_index in range(MB):
        hidden = signal[micro_index]
        stacked = []
        for layer_index in range(LAYERS):
            hidden = one_layer(hidden, head_proj[layer_index], record_start[micro_index], record_pad[micro_index])
            stacked.append(hidden)
        results.append(jnp.stack(stacked))
    return jnp.stack(results, axis=1)
```

```python
import math

import jax
import jax.numpy as jnp
from jax import lax
from jax.experimental import pallas as pl
from jax.experimental.pallas import tpu as pltpu
from jax.sharding import PartitionSpec as P

HEADS = 32
HEAD = 128
REACH = 4
MESH = pl.DeviceIdType.MESH
F32 = jnp.float32
BF16 = jnp.bfloat16
GROUP = 4
MASKED = -1e30


def kernel(
    sig_hbm, w_hbm, start_hbm, pad_hbm, out,
    sig, hid, w, start, pad, qkv, halo_kv, pin, pout, bias_t, bias_s,
    in_sem, own_s, own_r, halo_s, halo_r, p_s, p_r,
):
    micro, own, width = out.shape
    heads = width // HEAD
    chunks = heads // GROUP
    half = own // 2
    sections = lax.axis_size("section")
    count = lax.axis_size("seq")
    s = lax.axis_index("section")
    j = lax.axis_index("seq")
    r = lax.axis_index("rep")
    left = jnp.maximum(j - 1, 0)
    right = jnp.minimum(j + 1, count - 1)
    has_left = j > 0
    has_right = j < count - 1
    other = 1 - r
    following = lax.rem(s + 1, sections)
    before = jnp.maximum(s - 1, 0)
    first = s == 0
    last = s == sections - 1

    w_copy = pltpu.make_async_copy(w_hbm, w, in_sem.at[0])
    sig_copy = pltpu.make_async_copy(sig_hbm, sig, in_sem.at[1])
    start_copy = pltpu.make_async_copy(start_hbm, start, in_sem.at[2])
    pad_copy = pltpu.make_async_copy(pad_hbm, pad, in_sem.at[3])
    sig_copy.start()
    w_copy.start()
    start_copy.start()
    pad_copy.start()

    barrier = pltpu.get_barrier_semaphore()

    def greet(device):
        pl.semaphore_signal(barrier, inc=1, device_id=device, device_id_type=MESH)

    greet((before, j, other))

    @pl.when(has_left)
    def _():
        greet((s, left, r))
        greet((before, left, other))

    @pl.when(has_right)
    def _():
        greet((s, right, r))
        greet((before, right, other))

    @pl.when(jnp.logical_not(first))
    def _():
        greet((before, j, r))

    def lanes(c):
        return pl.ds(c * GROUP * HEAD, GROUP * HEAD)

    def own_copy(m, c):
        return pltpu.make_async_remote_copy(
            src_ref=out.at[m, :, lanes(c)],
            dst_ref=hid.at[m, pl.ds(0, own), lanes(c)],
            send_sem=own_s.at[m, c],
            recv_sem=own_r.at[m, c],
            device_id=(following, j, r),
            device_id_type=MESH,
        )

    def halo_copy(m, c, side):
        return pltpu.make_async_remote_copy(
            src_ref=hid.at[m, pl.ds(side * half, half), lanes(c)],
            dst_ref=hid.at[m, pl.ds(own + (1 - side) * half, half), lanes(c)],
            send_sem=halo_s.at[m, c, side],
            recv_sem=halo_r.at[m, c, side],
            device_id=(s, right if side else left, r),
            device_id_type=MESH,
        )

    def p_copy(k, m, section, i):
        src, dst, place = (
            (pl.ds(0, half), pl.ds(own + half, half), left),
            (pl.ds(half, half), pl.ds(own, half), right),
            (pl.ds(0, own), pl.ds(0, own), j),
        )[i]
        return pltpu.make_async_remote_copy(
            src_ref=pout.at[k, m, src],
            dst_ref=pin.at[m, dst],
            send_sem=p_s.at[k, m, i],
            recv_sem=p_r.at[m, i],
            device_id=(section, place, other),
            device_id_type=MESH,
        )

    def sides(to_left, to_right):
        @pl.when(has_left)
        def _():
            to_left()

        @pl.when(has_right)
        def _():
            to_right()

    def forward_halo(m, c):
        sides(lambda: halo_copy(m, c, 0).start(), lambda: halo_copy(m, c, 1).start())

    def send_p(k, m, section):
        p_copy(k, m, section, 2).start()
        sides(
            lambda: p_copy(k, m, section, 0).start(),
            lambda: p_copy(k, m, section, 1).start(),
        )

    def wait_sent_p(k, m, section):
        p_copy(k, m, section, 2).wait_send()
        sides(
            lambda: p_copy(k, m, section, 0).wait_send(),
            lambda: p_copy(k, m, section, 1).wait_send(),
        )

    def squares(m, rows, heads_of):
        total = None
        for h in heads_of:
            x = hid[m, rows, h * HEAD : (h + 1) * HEAD].astype(F32)
            total = x * x if total is None else total + x * x
        return total

    every = range(heads)

    @pl.when(jnp.logical_not(has_left))
    def _():
        hid[:, pl.ds(own, half), :] = jnp.zeros((micro, half, width), BF16)
        pin[:, pl.ds(own, half), :] = jnp.zeros((micro, half, HEAD), F32)

    @pl.when(jnp.logical_not(has_right))
    def _():
        hid[:, pl.ds(own + half, half), :] = jnp.zeros((micro, half, width), BF16)
        pin[:, pl.ds(own + half, half), :] = jnp.zeros((micro, half, HEAD), F32)

    sig_copy.wait()

    @pl.when(first)
    def _():
        for m in range(micro):
            partial = jnp.zeros((own, HEAD), F32)
            for h in every:
                x = sig[m, :, :, h * HEAD : (h + 1) * HEAD].astype(F32).reshape(own, HEAD)
                partial = partial + x * x
                hid[m, pl.ds(0, own), h * HEAD : (h + 1) * HEAD] = x.astype(BF16)
            pout[0, m] = partial

    beside = has_left.astype(jnp.int32) + has_right.astype(jnp.int32)
    receivers = beside + jnp.where(last, 0, 2 + beside) + jnp.where(first, 1 + beside, 0)
    pl.semaphore_wait(barrier, receivers)

    @pl.when(first)
    def _():
        for m in range(micro):
            send_p(0, m, s)
        for m in range(micro):
            for c in range(chunks):
                forward_halo(m, c)

    start_copy.wait()
    pad_copy.wait()
    row = lax.broadcasted_iota(jnp.int32, (2 * own, 4 * own), 0)
    col = lax.broadcasted_iota(jnp.int32, (2 * own, 4 * own), 1) & (own - 1)
    key_time = (row >> 2) - jnp.where(row < own, 0, jnp.where(row < own + half, 12, 4))
    key_station = row & 3
    query_time = col >> 2
    query_station = col & 3
    step = j * (own // 4) + key_time
    total_steps = count * (own // 4)
    for m in range(micro):
        begin = jnp.zeros_like(row)
        end = jnp.zeros_like(row)
        for z in range(4):
            begin = jnp.where(key_station == z, start[m, z], begin)
            end = jnp.where(key_station == z, total_steps - pad[m, z], end)
        valid = (step >= begin) & (step < end)
        same_time = key_time == query_time
        same_station = key_station == query_station
        near = jnp.abs(key_time - query_time) <= REACH
        bias_t[m] = jnp.where(same_station & near & (valid | same_time), 0.0, MASKED)
        keep = same_time & (valid | same_station)
        bias_s[m] = jnp.where(keep, 0.0, MASKED)[:own]

    w_copy.wait()
    scale = math.log2(math.e) / math.sqrt(HEAD)

    def inverse(m, rows):
        total = jnp.sum(squares(m, rows, every) + pin[m, rows], axis=-1, keepdims=True)
        return jnp.broadcast_to(lax.rsqrt(total / (HEADS * HEAD) + 1e-06), (own, HEAD))

    def normed(m, rows, h, inv):
        x = hid[m, rows, h * HEAD : (h + 1) * HEAD]
        return (x.astype(F32) * inv).astype(BF16)

    @pl.loop(0, micro)
    def _(m):
        @pl.when(jnp.logical_not(first))
        def _():
            for c in range(chunks):
                own_copy(m, c).wait_recv()
                forward_halo(m, c)

        p_copy(1, m, following, 2).wait_recv()
        inv = inverse(m, pl.ds(0, own))
        for h in every:
            x = normed(m, pl.ds(0, own), h, inv)
            qkv[h] = jnp.dot(x, w[h], preferred_element_type=F32).astype(BF16)

        def arrived(side):
            p_copy(1, m, following, side).wait_recv()
            for c in range(chunks):
                halo_copy(m, c, side).wait_recv()

        sides(lambda: arrived(1), lambda: arrived(0))
        inv = inverse(m, pl.ds(own, own))
        for h in every:
            x = normed(m, pl.ds(own, own), h, inv)
            halo_kv[h] = jnp.dot(x, w[h, :, HEAD:], preferred_element_type=F32).astype(BF16)
        sent = jnp.zeros((own, HEAD), F32)
        for c in range(chunks):
            queries, keys, values = [], [], []
            blank = jnp.zeros((own, HEAD), BF16)
            for i in range(GROUP):
                h = c * GROUP + i
                q = qkv[h, :, :HEAD]
                queries.append(
                    jnp.concatenate([q if i == n else blank for n in range(GROUP)], axis=1)
                )
                k = qkv[h, :, HEAD : 2 * HEAD]
                keys.append(jnp.concatenate([k, halo_kv[h, :, :HEAD]], axis=0))
                v = qkv[h, :, 2 * HEAD :]
                values.append(jnp.concatenate([v, halo_kv[h, :, HEAD:], v], axis=0))
            scores = lax.dot_general(
                jnp.concatenate(keys, axis=1),
                jnp.concatenate(queries, axis=0),
                (((1,), (1,)), ((), ())),
                preferred_element_type=F32,
            ) * scale
            along = scores + bias_t[m]
            along = jnp.exp2(along - jnp.max(along, axis=0, keepdims=True))
            along = along * (1.0 / jnp.sum(along, axis=0, keepdims=True))
            across = scores[:own] + bias_s[m]
            across = jnp.exp2(across - jnp.max(across, axis=0, keepdims=True))
            across = across * (1.0 / jnp.sum(across, axis=0, keepdims=True))
            mix = jnp.transpose(jnp.concatenate([along, across], axis=0)).astype(BF16)
            for i in range(GROUP):
                h = c * GROUP + i
                update = jnp.dot(
                    mix[i * own : (i + 1) * own], values[i], preferred_element_type=F32
                )
                x = hid[m, pl.ds(0, own), h * HEAD : (h + 1) * HEAD].astype(F32)
                y = (x + update).astype(BF16)
                out[m, :, h * HEAD : (h + 1) * HEAD] = y
                y = y.astype(F32)
                sent = sent + y * y

            @pl.when(jnp.logical_not(last))
            def _():
                own_copy(m, c).start()

        @pl.when(jnp.logical_not(last))
        def _():
            pout[1, m] = sent
            send_p(1, m, following)

    def sent_halo(side):
        for m in range(micro):
            for c in range(chunks):
                halo_copy(m, c, side).wait_send()

    sides(lambda: sent_halo(0), lambda: sent_halo(1))

    @pl.when(first)
    def _():
        for m in range(micro):
            wait_sent_p(0, m, s)

    @pl.when(jnp.logical_not(last))
    def _():
        for m in range(micro):
            for c in range(chunks):
                own_copy(m, c).wait_send()
            wait_sent_p(1, m, following)


def body(signal, head_proj, record_start, record_pad):
    micro, times, stations, width = signal.shape
    own = times * stations
    heads = width // HEAD
    chunks = heads // GROUP
    dma = pltpu.SemaphoreType.DMA
    vmem = pl.BlockSpec(memory_space=pltpu.VMEM)
    hbm = pl.BlockSpec(memory_space=pltpu.HBM)
    result = pl.pallas_call(
        kernel,
        name="relay",
        out_shape=jax.ShapeDtypeStruct((micro, own, width), BF16),
        in_specs=[hbm] * 4,
        out_specs=vmem,
        scratch_shapes=[
            pltpu.VMEM(signal.shape, BF16),
            pltpu.VMEM((micro, 2 * own, width), BF16),
            pltpu.VMEM((heads, HEAD, 3 * HEAD), BF16),
            pltpu.SMEM(record_start.shape, jnp.int32),
            pltpu.SMEM(record_pad.shape, jnp.int32),
            pltpu.VMEM((heads, own, 3 * HEAD), BF16),
            pltpu.VMEM((heads, own, 2 * HEAD), BF16),
            pltpu.VMEM((micro, 2 * own, HEAD), F32),
            pltpu.VMEM((2, micro, own, HEAD), F32),
            pltpu.VMEM((micro, 2 * own, 4 * own), F32),
            pltpu.VMEM((micro, own, 4 * own), F32),
            dma((4,)),
            dma((micro, chunks)),
            dma((micro, chunks)),
            dma((micro, chunks, 2)),
            dma((micro, chunks, 2)),
            dma((2, micro, 3)),
            dma((micro, 3)),
        ],
        compiler_params=pltpu.CompilerParams(
            collective_id=0, has_side_effects=True, vmem_limit_bytes=40 * 2**20
        ),
    )(*[pltpu.with_memory_space_constraint(x, pltpu.HBM) for x in (signal, head_proj[0], record_start, record_pad)])
    return result.reshape(1, micro, times, stations, width)


def solution(mesh):
    return jax.shard_map(
        body,
        mesh=mesh,
        in_specs=(P(None, "seq", None, "rep"), P("section", "rep", None, None), P(), P()),
        out_specs=P("section", None, "seq", None, "rep"),
        check_vma=False,
    )
```

```python
import math

import jax
import jax.numpy as jnp
from jax import lax
from jax.experimental import pallas as pl
from jax.experimental.pallas import tpu as pltpu
from jax.sharding import PartitionSpec as P

HEADS = 32
HEAD = 128
REACH = 4
MESH = pl.DeviceIdType.MESH
F32 = jnp.float32
BF16 = jnp.bfloat16
GROUP = 4
MASKED = -1e30


def kernel(
    sig_hbm, w_hbm, start_hbm, pad_hbm, out,
    sig, hid, w, start, pad, qkv, halo_kv, pin, pout, bias_t, bias_s,
    in_sem, own_s, own_r, halo_s, halo_r, p_s, p_r,
):
    micro, own, width = out.shape
    heads = width // HEAD
    chunks = heads // GROUP
    half = own // 2
    sections = lax.axis_size("section")
    count = lax.axis_size("seq")
    s = lax.axis_index("section")
    j = lax.axis_index("seq")
    r = lax.axis_index("rep")
    left = jnp.maximum(j - 1, 0)
    right = jnp.minimum(j + 1, count - 1)
    has_left = j > 0
    has_right = j < count - 1
    other = 1 - r
    following = lax.rem(s + 1, sections)
    before = jnp.maximum(s - 1, 0)
    first = s == 0
    last = s == sections - 1

    w_copy = pltpu.make_async_copy(w_hbm, w, in_sem.at[0])
    sig_copy = pltpu.make_async_copy(sig_hbm, sig, in_sem.at[1])
    start_copy = pltpu.make_async_copy(start_hbm, start, in_sem.at[2])
    pad_copy = pltpu.make_async_copy(pad_hbm, pad, in_sem.at[3])
    sig_copy.start()
    w_copy.start()
    start_copy.start()
    pad_copy.start()

    barrier = pltpu.get_barrier_semaphore()

    def greet(device):
        pl.semaphore_signal(barrier, inc=1, device_id=device, device_id_type=MESH)

    greet((before, j, other))

    @pl.when(has_left)
    def _():
        greet((s, left, r))
        greet((before, left, other))

    @pl.when(has_right)
    def _():
        greet((s, right, r))
        greet((before, right, other))

    @pl.when(jnp.logical_not(first))
    def _():
        greet((before, j, r))

        @pl.when(has_left)
        def _():
            greet((before, left, r))

        @pl.when(has_right)
        def _():
            greet((before, right, r))

    def lanes(c):
        return pl.ds(c * GROUP * HEAD, GROUP * HEAD)

    def own_copy(m, c):
        return pltpu.make_async_remote_copy(
            src_ref=out.at[m, :, lanes(c)],
            dst_ref=hid.at[m, pl.ds(0, own), lanes(c)],
            send_sem=own_s.at[m, c],
            recv_sem=own_r.at[m, c],
            device_id=(following, j, r),
            device_id_type=MESH,
        )

    def halo_copy(m, c, side):
        return pltpu.make_async_remote_copy(
            src_ref=hid.at[m, pl.ds(side * half, half), lanes(c)],
            dst_ref=hid.at[m, pl.ds(own + (1 - side) * half, half), lanes(c)],
            send_sem=halo_s.at[m, c, side],
            recv_sem=halo_r.at[m, c, side],
            device_id=(s, right if side else left, r),
            device_id_type=MESH,
        )

    def p_copy(k, m, section, i, rep):
        src, dst, place = (
            (pl.ds(0, half), pl.ds(own + half, half), left),
            (pl.ds(half, half), pl.ds(own, half), right),
            (pl.ds(0, own), pl.ds(0, own), j),
        )[i]
        return pltpu.make_async_remote_copy(
            src_ref=pout.at[k, m, src],
            dst_ref=pin.at[rep, m, dst],
            send_sem=p_s.at[k, m, i, rep],
            recv_sem=p_r.at[m, i, rep],
            device_id=(section, place, other if rep else r),
            device_id_type=MESH,
        )

    def sides(to_left, to_right):
        @pl.when(has_left)
        def _():
            to_left()

        @pl.when(has_right)
        def _():
            to_right()

    def forward_halo(m, c):
        sides(lambda: halo_copy(m, c, 0).start(), lambda: halo_copy(m, c, 1).start())

    def send_p(k, m, section):
        p_copy(k, m, section, 2, 1).start()
        for rep in (1, 0):
            sides(
                lambda: p_copy(k, m, section, 0, rep).start(),
                lambda: p_copy(k, m, section, 1, rep).start(),
            )

    def wait_sent_p(k, m, section):
        p_copy(k, m, section, 2, 1).wait_send()
        for rep in (1, 0):
            sides(
                lambda: p_copy(k, m, section, 0, rep).wait_send(),
                lambda: p_copy(k, m, section, 1, rep).wait_send(),
            )

    def squares(m, rows, heads_of):
        total = None
        for h in heads_of:
            x = hid[m, rows, h * HEAD : (h + 1) * HEAD].astype(F32)
            total = x * x if total is None else total + x * x
        return total

    every = range(heads)

    @pl.when(jnp.logical_not(has_left))
    def _():
        hid[:, pl.ds(own, half), :] = jnp.zeros((micro, half, width), BF16)
        pin[:, :, pl.ds(own, half), :] = jnp.zeros((2, micro, half, HEAD), F32)

    @pl.when(jnp.logical_not(has_right))
    def _():
        hid[:, pl.ds(own + half, half), :] = jnp.zeros((micro, half, width), BF16)
        pin[:, :, pl.ds(own + half, half), :] = jnp.zeros((2, micro, half, HEAD), F32)

    sig_copy.wait()

    @pl.when(first)
    def _():
        for m in range(micro):
            partial = jnp.zeros((own, HEAD), F32)
            for h in every:
                x = sig[m, :, :, h * HEAD : (h + 1) * HEAD].astype(F32).reshape(own, HEAD)
                partial = partial + x * x
                hid[m, pl.ds(0, own), h * HEAD : (h + 1) * HEAD] = x.astype(BF16)
            pout[0, m] = partial

    beside = has_left.astype(jnp.int32) + has_right.astype(jnp.int32)
    receivers = beside + jnp.where(last, 0, 2 + 2 * beside) + jnp.where(first, 1 + beside, 0)
    pl.semaphore_wait(barrier, receivers)

    @pl.when(first)
    def _():
        for m in range(micro):
            send_p(0, m, s)
        for m in range(micro):
            for c in range(chunks):
                forward_halo(m, c)

    start_copy.wait()
    pad_copy.wait()
    row = lax.broadcasted_iota(jnp.int32, (2 * own, 4 * own), 0)
    col = lax.broadcasted_iota(jnp.int32, (2 * own, 4 * own), 1) & (own - 1)
    key_time = (row >> 2) - jnp.where(row < own, 0, jnp.where(row < own + half, 12, 4))
    key_station = row & 3
    query_time = col >> 2
    query_station = col & 3
    step = j * (own // 4) + key_time
    total_steps = count * (own // 4)
    for m in range(micro):
        begin = jnp.zeros_like(row)
        end = jnp.zeros_like(row)
        for z in range(4):
            begin = jnp.where(key_station == z, start[m, z], begin)
            end = jnp.where(key_station == z, total_steps - pad[m, z], end)
        valid = (step >= begin) & (step < end)
        same_time = key_time == query_time
        same_station = key_station == query_station
        near = jnp.abs(key_time - query_time) <= REACH
        bias_t[m] = jnp.where(same_station & near & (valid | same_time), 0.0, MASKED)
        keep = same_time & (valid | same_station)
        bias_s[m] = jnp.where(keep, 0.0, MASKED)[:own]

    w_copy.wait()
    scale = math.log2(math.e) / math.sqrt(HEAD)

    def inverse(total):
        total = jnp.sum(total, axis=-1, keepdims=True)
        return jnp.broadcast_to(lax.rsqrt(total / (HEADS * HEAD) + 1e-06), (own, HEAD))

    def normed(m, rows, h, inv):
        x = hid[m, rows, h * HEAD : (h + 1) * HEAD]
        return (x.astype(F32) * inv).astype(BF16)

    @pl.when(jnp.logical_not(first))
    def _():
        for c in range(chunks):
            own_copy(0, c).wait_recv()
            forward_halo(0, c)

    near = pl.ds(0, own)
    beyond = pl.ds(own, own)

    @pl.loop(0, micro)
    def _(m):
        mine = squares(m, near, every)
        p_copy(1, m, following, 2, 1).wait_recv()
        inv = inverse(mine + pin[1, m, near])
        for h in every:
            x = normed(m, near, h, inv)
            qkv[h] = jnp.dot(x, w[h], preferred_element_type=F32).astype(BF16)
        for rep in (1, 0):
            sides(
                lambda: p_copy(1, m, following, 1, rep).wait_recv(),
                lambda: p_copy(1, m, following, 0, rep).wait_recv(),
            )
        inv = inverse(pin[0, m, beyond] + pin[1, m, beyond])
        sent = jnp.zeros((own, HEAD), F32)
        for c in range(chunks):
            @pl.when(jnp.logical_not(first) & (m + 1 < micro))
            def _():
                own_copy(m + 1, c).wait_recv()
                forward_halo(m + 1, c)

            sides(
                lambda: halo_copy(m, c, 1).wait_recv(),
                lambda: halo_copy(m, c, 0).wait_recv(),
            )
            for h in range(c * GROUP, (c + 1) * GROUP):
                x = normed(m, beyond, h, inv)
                halo_kv[h] = jnp.dot(x, w[h, :, HEAD:], preferred_element_type=F32).astype(BF16)
            queries, keys, values = [], [], []
            blank = jnp.zeros((own, HEAD), BF16)
            for i in range(GROUP):
                h = c * GROUP + i
                q = qkv[h, :, :HEAD]
                queries.append(
                    jnp.concatenate([q if i == n else blank for n in range(GROUP)], axis=1)
                )
                k = qkv[h, :, HEAD : 2 * HEAD]
                keys.append(jnp.concatenate([k, halo_kv[h, :, :HEAD]], axis=0))
                v = qkv[h, :, 2 * HEAD :]
                values.append(jnp.concatenate([v, halo_kv[h, :, HEAD:], v], axis=0))
            scores = lax.dot_general(
                jnp.concatenate(keys, axis=1),
                jnp.concatenate(queries, axis=0),
                (((1,), (1,)), ((), ())),
                preferred_element_type=F32,
            ) * scale
            along = scores + bias_t[m]
            along = jnp.exp2(along - jnp.max(along, axis=0, keepdims=True))
            along = along * (1.0 / jnp.sum(along, axis=0, keepdims=True))
            across = scores[:own] + bias_s[m]
            across = jnp.exp2(across - jnp.max(across, axis=0, keepdims=True))
            across = across * (1.0 / jnp.sum(across, axis=0, keepdims=True))
            mix = jnp.transpose(jnp.concatenate([along, across], axis=0)).astype(BF16)
            for i in range(GROUP):
                h = c * GROUP + i
                update = jnp.dot(
                    mix[i * own : (i + 1) * own], values[i], preferred_element_type=F32
                )
                x = hid[m, pl.ds(0, own), h * HEAD : (h + 1) * HEAD].astype(F32)
                y = (x + update).astype(BF16)
                out[m, :, h * HEAD : (h + 1) * HEAD] = y
                y = y.astype(F32)
                sent = sent + y * y

            @pl.when(jnp.logical_not(last))
            def _():
                own_copy(m, c).start()

        @pl.when(jnp.logical_not(last))
        def _():
            pout[1, m] = sent
            send_p(1, m, following)

    def sent_halo(side):
        for m in range(micro):
            for c in range(chunks):
                halo_copy(m, c, side).wait_send()

    sides(lambda: sent_halo(0), lambda: sent_halo(1))

    @pl.when(first)
    def _():
        for m in range(micro):
            wait_sent_p(0, m, s)

    @pl.when(jnp.logical_not(last))
    def _():
        for m in range(micro):
            for c in range(chunks):
                own_copy(m, c).wait_send()
            wait_sent_p(1, m, following)


def body(signal, head_proj, record_start, record_pad):
    micro, times, stations, width = signal.shape
    own = times * stations
    heads = width // HEAD
    chunks = heads // GROUP
    dma = pltpu.SemaphoreType.DMA
    vmem = pl.BlockSpec(memory_space=pltpu.VMEM)
    hbm = pl.BlockSpec(memory_space=pltpu.HBM)
    result = pl.pallas_call(
        kernel,
        name="relay",
        out_shape=jax.ShapeDtypeStruct((micro, own, width), BF16),
        in_specs=[hbm] * 4,
        out_specs=vmem,
        scratch_shapes=[
            pltpu.VMEM(signal.shape, BF16),
            pltpu.VMEM((micro, 2 * own, width), BF16),
            pltpu.VMEM((heads, HEAD, 3 * HEAD), BF16),
            pltpu.SMEM(record_start.shape, jnp.int32),
            pltpu.SMEM(record_pad.shape, jnp.int32),
            pltpu.VMEM((heads, own, 3 * HEAD), BF16),
            pltpu.VMEM((heads, own, 2 * HEAD), BF16),
            pltpu.VMEM((2, micro, 2 * own, HEAD), F32),
            pltpu.VMEM((2, micro, own, HEAD), F32),
            pltpu.VMEM((micro, 2 * own, 4 * own), F32),
            pltpu.VMEM((micro, own, 4 * own), F32),
            dma((4,)),
            dma((micro, chunks)),
            dma((micro, chunks)),
            dma((micro, chunks, 2)),
            dma((micro, chunks, 2)),
            dma((2, micro, 3, 2)),
            dma((micro, 3, 2)),
        ],
        compiler_params=pltpu.CompilerParams(
            collective_id=0, has_side_effects=True, vmem_limit_bytes=40 * 2**20
        ),
    )(*[pltpu.with_memory_space_constraint(x, pltpu.HBM) for x in (signal, head_proj[0], record_start, record_pad)])
    return result.reshape(1, micro, times, stations, width)


def solution(mesh):
    return jax.shard_map(
        body,
        mesh=mesh,
        in_specs=(P(None, "seq", None, "rep"), P("section", "rep", None, None), P(), P()),
        out_specs=P("section", None, "seq", None, "rep"),
        check_vma=False,
    )
```

```python
import math

import jax
import jax.numpy as jnp
from jax import lax
from jax.experimental import pallas as pl
from jax.experimental.pallas import tpu as pltpu
from jax.sharding import PartitionSpec as P

HEADS = 32
HEAD = 128
REACH = 4
MESH = pl.DeviceIdType.MESH
F32 = jnp.float32
BF16 = jnp.bfloat16
GROUP = 4
MASKED = -1e30


def kernel(
    sig_hbm, w_hbm, start_hbm, pad_hbm, out,
    sig, hid, w, start, pad, qkv, halo_kv, pin, pout, res, bias_t, bias_s,
    in_sem, own_s, own_r, halo_s, halo_r, p_s, p_r, seed_s, seed_r, seed_h, end_s, end_r, ready,
):
    micro, own, width = out.shape
    heads = width // HEAD
    chunks = heads // GROUP
    half = own // 2
    sections = lax.axis_size("section")
    count = lax.axis_size("seq")
    s = lax.axis_index("section")
    j = lax.axis_index("seq")
    r = lax.axis_index("rep")
    other = 1 - r
    following = lax.rem(s + 1, sections)
    before = jnp.maximum(s - 1, 0)
    first = s == 0
    last = s == sections - 1

    late = first & (j == 0) & (r == 0)
    helper = first & (j == 1) & (r == 0)
    donor = (s == 1) & (j == 0) & (r == 0)
    active = jnp.logical_not(late)

    def number(flag):
        return flag.astype(jnp.int32)

    def sides(to_left, to_right, tile=0):
        at = j - tile

        @pl.when(at > 0)
        def _():
            to_left()

        @pl.when(at < count - 1)
        def _():
            to_right()

    w_copy = pltpu.make_async_copy(w_hbm, w, in_sem.at[0])
    sig_copy = pltpu.make_async_copy(sig_hbm, sig, in_sem.at[1])
    start_copy = pltpu.make_async_copy(start_hbm, start, in_sem.at[2])
    pad_copy = pltpu.make_async_copy(pad_hbm, pad, in_sem.at[3])
    sig_copy.start()
    w_copy.start()
    start_copy.start()
    pad_copy.start()

    barrier = pltpu.get_barrier_semaphore()

    def signal(device):
        pl.semaphore_signal(barrier, inc=1, device_id=device, device_id_type=MESH)

    def greet(section, place, rep):
        is_late = (section == 0) & (place == 0) & (rep == 0)

        @pl.when(jnp.logical_not(is_late & (s == 1)))
        def _():
            signal((section + number(is_late), place, rep))

    left = jnp.maximum(j - 1, 0)
    right = jnp.minimum(j + 1, count - 1)
    has_left = j > 0
    has_right = j < count - 1

    @pl.when(active)
    def _():
        greet(before, j, other)
        sides(lambda: greet(s, left, r), lambda: greet(s, right, r))
        sides(lambda: greet(before, left, other), lambda: greet(before, right, other))

        @pl.when(jnp.logical_not(first))
        def _():
            greet(before, j, r)
            sides(lambda: greet(before, left, r), lambda: greet(before, right, r))

    @pl.when(helper)
    def _():
        signal((s, left, r))

    def lanes(c):
        return pl.ds(c * GROUP * HEAD, GROUP * HEAD)

    def own_copy(t, m, c):
        return pltpu.make_async_remote_copy(
            src_ref=res.at[t, m, :, lanes(c)],
            dst_ref=hid.at[0, m, pl.ds(0, own), lanes(c)],
            send_sem=own_s.at[t, m, c],
            recv_sem=own_r.at[m, c],
            device_id=(following, j - t, r),
            device_id_type=MESH,
        )

    def halo_copy(m, c, side):
        return pltpu.make_async_remote_copy(
            src_ref=hid.at[0, m, pl.ds(side * half, half), lanes(c)],
            dst_ref=hid.at[0, m, pl.ds(own + (1 - side) * half, half), lanes(c)],
            send_sem=halo_s.at[m, c, side],
            recv_sem=halo_r.at[m, c, side],
            device_id=(s, right if side else left, r),
            device_id_type=MESH,
        )

    def seed_copy(m):
        return pltpu.make_async_remote_copy(
            src_ref=res.at[1, m],
            dst_ref=hid.at[1, m, pl.ds(0, own)],
            send_sem=seed_s.at[m],
            recv_sem=seed_r.at[m],
            device_id=(before, right, r),
            device_id_type=MESH,
        )

    def seed_halo_copy(m, c):
        return pltpu.make_async_remote_copy(
            src_ref=res.at[1, m, pl.ds(half, half), lanes(c)],
            dst_ref=hid.at[0, m, pl.ds(own, half), lanes(c)],
            send_sem=seed_h.at[m, c],
            recv_sem=halo_r.at[m, c, 1],
            device_id=(before, right, r),
            device_id_type=MESH,
        )

    def end_copy(m):
        return pltpu.make_async_remote_copy(
            src_ref=res.at[1, m],
            dst_ref=out.at[m],
            send_sem=end_s.at[m],
            recv_sem=end_r.at[m],
            device_id=(s, left, r),
            device_id_type=MESH,
        )

    def rows_of(i):
        return (
            (pl.ds(0, half), pl.ds(own + half, half)),
            (pl.ds(half, half), pl.ds(own, half)),
            (pl.ds(0, own), pl.ds(0, own)),
        )[i]

    def p_copy(k, t, m, section, i, rep):
        src, dst = rows_of(i)
        at = j - t
        place = (jnp.maximum(at - 1, 0), jnp.minimum(at + 1, count - 1), at)[i]
        to = other if rep else r
        moved = number((section == 0) & (place == 0) & (to == 0))
        return pltpu.make_async_remote_copy(
            src_ref=pout.at[k, t, m, src],
            dst_ref=pin.at[moved, rep, m, dst],
            send_sem=p_s.at[k, t, m, i, rep],
            recv_sem=p_r.at[moved, m, i, rep],
            device_id=(section, place + moved, to),
            device_id_type=MESH,
        )

    def p_arrived(t, m, i, rep):
        src, dst = rows_of(i)
        pltpu.make_async_remote_copy(
            src_ref=pout.at[0, 0, m, src],
            dst_ref=pin.at[t, rep, m, dst],
            send_sem=p_s.at[0, 0, m, i, rep],
            recv_sem=p_r.at[t, m, i, rep],
            device_id=(s, j, other),
            device_id_type=MESH,
        ).wait_recv()

    def forward_halo(m, c):
        @pl.when(jnp.logical_not(helper))
        def _():
            sides(lambda: halo_copy(m, c, 0).start(), lambda: None)

        sides(lambda: None, lambda: halo_copy(m, c, 1).start())

    def each_p(k, t, m, section, act):
        act(p_copy(k, t, m, section, 2, 1))
        sides(
            lambda: act(p_copy(k, t, m, section, 0, 1)),
            lambda: act(p_copy(k, t, m, section, 1, 1)),
            t,
        )

        def to_left():
            if k:
                act(p_copy(k, t, m, section, 0, 0))
            else:
                @pl.when(jnp.logical_not(helper))
                def _():
                    act(p_copy(k, t, m, section, 0, 0))

        sides(to_left, lambda: act(p_copy(k, t, m, section, 1, 0)), t)

    def squares(t, m, rows, heads_of):
        total = None
        for h in heads_of:
            x = hid[t, m, rows, h * HEAD : (h + 1) * HEAD].astype(F32)
            total = x * x if total is None else total + x * x
        return total

    every = range(heads)

    def clear(t, rows):
        hid[t, :, rows, :] = jnp.zeros((micro, half, width), BF16)
        pin[t, :, :, rows, :] = jnp.zeros((2, micro, half, HEAD), F32)

    before_own, after_own = pl.ds(own, half), pl.ds(own + half, half)
    sides_missing = (jnp.logical_not(has_left), jnp.logical_not(has_right))

    @pl.when(sides_missing[0] & active)
    def _():
        clear(0, before_own)

    @pl.when(sides_missing[1])
    def _():
        clear(0, after_own)

    @pl.when(helper)
    def _():
        clear(1, before_own)

    sig_copy.wait()

    def relaid(store):
        for m in range(micro):
            partial = jnp.zeros((own, HEAD), F32)
            for h in every:
                cols = slice(h * HEAD, (h + 1) * HEAD)
                x = sig[m, :, :, cols].astype(F32).reshape(own, HEAD)
                partial = partial + x * x
                store(m, cols, x.astype(BF16))
            pout[0, 0, m] = partial

    @pl.when(first & active)
    def _():
        def store(m, cols, x):
            hid[0, m, pl.ds(0, own), cols] = x

        relaid(store)

    @pl.when(donor)
    def _():
        def store(m, cols, x):
            res[1, m, :, cols] = x

        relaid(store)

    @pl.when(helper)
    def _():
        for m in range(micro):
            hid[1, m, after_own, :] = hid[0, m, pl.ds(0, half), :]
            pin[1, 0, m, after_own] = pout[0, 0, m, pl.ds(0, half)]

    beside = number(has_left) + number(has_right)
    receivers = beside + jnp.where(last, 0, 2 + 2 * beside) + jnp.where(first, 1 + beside, 0)
    fewer = number(helper) + number(first & (j <= 1) & (r == 1))
    receivers = receivers - fewer + 3 * number(donor)
    pl.semaphore_wait(barrier, jnp.where(late, 1, receivers))

    @pl.when(late)
    def _():
        pl.semaphore_signal(ready, inc=1, device_id=(s, right, r), device_id_type=MESH)

    @pl.when((first & active) | donor)
    def _():
        for m in range(micro):
            each_p(0, 0, m, 0, lambda copy: copy.start())

    @pl.when(first & active)
    def _():
        for m in range(micro):
            for c in range(chunks):
                forward_halo(m, c)

    @pl.when(donor)
    def _():
        for m in range(micro):
            for c in range(chunks):
                seed_halo_copy(m, c).start()
            seed_copy(m).start()

    start_copy.wait()
    pad_copy.wait()

    row = lax.broadcasted_iota(jnp.int32, (2 * own, 4 * own), 0)
    col = lax.broadcasted_iota(jnp.int32, (2 * own, 4 * own), 1) & (own - 1)
    key_time = (row >> 2) - jnp.where(row < own, 0, jnp.where(row < own + half, 12, 4))
    key_station = row & 3
    query_time = col >> 2
    query_station = col & 3
    total_steps = count * (own // 4)
    same_time = key_time == query_time
    same_station = key_station == query_station
    close = jnp.abs(key_time - query_time) <= REACH

    def set_bias(t):
        step = (j - t) * (own // 4) + key_time
        for m in range(micro):
            begin = jnp.zeros_like(row)
            end = jnp.zeros_like(row)
            for z in range(4):
                begin = jnp.where(key_station == z, start[m, z], begin)
                end = jnp.where(key_station == z, total_steps - pad[m, z], end)
            valid = (step >= begin) & (step < end)
            keep = same_station & close & (valid | same_time)
            bias_t[t, m] = jnp.where(keep, 0.0, MASKED)
            keep = same_time & (valid | same_station)
            bias_s[t, m] = jnp.where(keep, 0.0, MASKED)[:own]

    set_bias(0)

    @pl.when(helper)
    def _():
        set_bias(1)

    w_copy.wait()
    scale = math.log2(math.e) / math.sqrt(HEAD)

    def inverse(total):
        total = jnp.sum(total, axis=-1, keepdims=True)
        return jnp.broadcast_to(lax.rsqrt(total / (HEADS * HEAD) + 1e-06), (own, HEAD))

    def normed(t, m, rows, h, inv):
        x = hid[t, m, rows, h * HEAD : (h + 1) * HEAD]
        return (x.astype(F32) * inv).astype(BF16)

    @pl.when(jnp.logical_not(first))
    def _():
        for c in range(chunks):
            own_copy(0, 0, c).wait_recv()
            forward_halo(0, c)

    near = pl.ds(0, own)
    beyond = pl.ds(own, own)

    tiles = 1 + number(helper)

    @pl.loop(0, jnp.where(late, 0, micro * tiles))
    def _(turn):
        m = turn // tiles
        t = turn % tiles

        @pl.when(t == 1)
        def _():
            seed_copy(m).wait_recv()

        mine = squares(t, m, near, every)
        p_arrived(t, m, 2, 1)
        inv = inverse(mine + pin[t, 1, m, near])
        for h in every:
            x = normed(t, m, near, h, inv)
            qkv[h] = jnp.dot(x, w[h], preferred_element_type=F32).astype(BF16)
        sides(lambda: p_arrived(t, m, 1, 1), lambda: p_arrived(t, m, 0, 1), t)

        @pl.when(t == 0)
        def _():
            sides(lambda: p_arrived(0, m, 1, 0), lambda: p_arrived(0, m, 0, 0))

        inv = inverse(pin[t, 0, m, beyond] + pin[t, 1, m, beyond])
        sent = jnp.zeros((own, HEAD), F32)
        for c in range(chunks):
            @pl.when(jnp.logical_not(first) & (m + 1 < micro))
            def _():
                own_copy(0, m + 1, c).wait_recv()
                forward_halo(m + 1, c)

            @pl.when(t == 0)
            def _():
                sides(
                    lambda: halo_copy(m, c, 1).wait_recv(),
                    lambda: halo_copy(m, c, 0).wait_recv(),
                )

            for h in range(c * GROUP, (c + 1) * GROUP):
                x = normed(t, m, beyond, h, inv)
                halo_kv[h] = jnp.dot(x, w[h, :, HEAD:], preferred_element_type=F32).astype(BF16)
            queries, keys, values = [], [], []
            blank = jnp.zeros((own, HEAD), BF16)
            for i in range(GROUP):
                h = c * GROUP + i
                q = qkv[h, :, :HEAD]
                queries.append(
                    jnp.concatenate([q if i == n else blank for n in range(GROUP)], axis=1)
                )
                k = qkv[h, :, HEAD : 2 * HEAD]
                keys.append(jnp.concatenate([k, halo_kv[h, :, :HEAD]], axis=0))
                v = qkv[h, :, 2 * HEAD :]
                values.append(jnp.concatenate([v, halo_kv[h, :, HEAD:], v], axis=0))
            scores = lax.dot_general(
                jnp.concatenate(keys, axis=1),
                jnp.concatenate(queries, axis=0),
                (((1,), (1,)), ((), ())),
                preferred_element_type=F32,
            ) * scale
            along = scores + bias_t[t, m]
            along = jnp.exp2(along - jnp.max(along, axis=0, keepdims=True))
            along = along * (1.0 / jnp.sum(along, axis=0, keepdims=True))
            across = scores[:own] + bias_s[t, m]
            across = jnp.exp2(across - jnp.max(across, axis=0, keepdims=True))
            across = across * (1.0 / jnp.sum(across, axis=0, keepdims=True))
            mix = jnp.transpose(jnp.concatenate([along, across], axis=0)).astype(BF16)
            for i in range(GROUP):
                h = c * GROUP + i
                update = jnp.dot(
                    mix[i * own : (i + 1) * own], values[i], preferred_element_type=F32
                )
                x = hid[t, m, pl.ds(0, own), h * HEAD : (h + 1) * HEAD].astype(F32)
                y = (x + update).astype(BF16)
                res[t, m, :, h * HEAD : (h + 1) * HEAD] = y
                y = y.astype(F32)
                sent = sent + y * y

            @pl.when(jnp.logical_not(last))
            def _():
                own_copy(t, m, c).start()

        @pl.when(jnp.logical_not(last))
        def _():
            pout[1, t, m] = sent
            each_p(1, t, m, following, lambda copy: copy.start())

    @pl.when(active)
    def _():
        out[...] = res[0]

        @pl.when(jnp.logical_not(helper))
        def _():
            sides(
                lambda: [halo_copy(m, c, 0).wait_send() for m in range(micro) for c in range(chunks)],
                lambda: None,
            )

        sides(
            lambda: None,
            lambda: [halo_copy(m, c, 1).wait_send() for m in range(micro) for c in range(chunks)],
        )

    def wait_sent(t):
        for m in range(micro):
            for c in range(chunks):
                own_copy(t, m, c).wait_send()
            each_p(1, t, m, following, lambda copy: copy.wait_send())

    @pl.when(active & jnp.logical_not(last))
    def _():
        wait_sent(0)

    @pl.when((first & active) | donor)
    def _():
        for m in range(micro):
            each_p(0, 0, m, 0, lambda copy: copy.wait_send())

    @pl.when(donor)
    def _():
        for m in range(micro):
            for c in range(chunks):
                seed_halo_copy(m, c).wait_send()
            seed_copy(m).wait_send()

    @pl.when(helper)
    def _():
        wait_sent(1)
        pl.semaphore_wait(ready, 1)
        for m in range(micro):
            end_copy(m).start()
        for m in range(micro):
            end_copy(m).wait_send()

    @pl.when(late)
    def _():
        for m in range(micro):
            end_copy(m).wait_recv()


def body(signal, head_proj, record_start, record_pad):
    micro, times, stations, width = signal.shape
    own = times * stations
    heads = width // HEAD
    chunks = heads // GROUP
    dma = pltpu.SemaphoreType.DMA
    vmem = pl.BlockSpec(memory_space=pltpu.VMEM)
    hbm = pl.BlockSpec(memory_space=pltpu.HBM)
    result = pl.pallas_call(
        kernel,
        name="relay",
        out_shape=jax.ShapeDtypeStruct((micro, own, width), BF16),
        in_specs=[hbm] * 4,
        out_specs=vmem,
        scratch_shapes=[
            pltpu.VMEM(signal.shape, BF16),
            pltpu.VMEM((2, micro, 2 * own, width), BF16),
            pltpu.VMEM((heads, HEAD, 3 * HEAD), BF16),
            pltpu.SMEM(record_start.shape, jnp.int32),
            pltpu.SMEM(record_pad.shape, jnp.int32),
            pltpu.VMEM((heads, own, 3 * HEAD), BF16),
            pltpu.VMEM((heads, own, 2 * HEAD), BF16),
            pltpu.VMEM((2, 2, micro, 2 * own, HEAD), F32),
            pltpu.VMEM((2, 2, micro, own, HEAD), F32),
            pltpu.VMEM((2, micro, own, width), BF16),
            pltpu.VMEM((2, micro, 2 * own, 4 * own), F32),
            pltpu.VMEM((2, micro, own, 4 * own), F32),
            dma((4,)),
            dma((2, micro, chunks)),
            dma((micro, chunks)),
            dma((micro, chunks, 2)),
            dma((micro, chunks, 2)),
            dma((2, 2, micro, 3, 2)),
            dma((2, micro, 3, 2)),
            dma((micro,)),
            dma((micro,)),
            dma((micro, chunks)),
            dma((micro,)),
            dma((micro,)),
            pltpu.SemaphoreType.REGULAR,
        ],
        compiler_params=pltpu.CompilerParams(
            collective_id=0, has_side_effects=True, vmem_limit_bytes=40 * 2**20
        ),
    )(*[pltpu.with_memory_space_constraint(x, pltpu.HBM) for x in (signal, head_proj[0], record_start, record_pad)])
    return result.reshape(1, micro, times, stations, width)


def solution(mesh):
    return jax.shard_map(
        body,
        mesh=mesh,
        in_specs=(P(None, "seq", None, "rep"), P("section", "rep", None, None), P(), P()),
        out_specs=P("section", None, "seq", None, "rep"),
        check_vma=False,
    )
```

```python
import math

import jax
import jax.numpy as jnp
from jax import lax
from jax.experimental import pallas as pl
from jax.experimental.pallas import tpu as pltpu
from jax.sharding import PartitionSpec as P

HEADS = 32
HEAD = 128
REACH = 4
MESH = pl.DeviceIdType.MESH
F32 = jnp.float32
BF16 = jnp.bfloat16
GROUP = 4
BLOCKS = ((0,), (1,), (2,), (3,))
MASKED = -1e30


def kernel(
    sig_hbm, w_hbm, start_hbm, pad_hbm, out,
    sig, hid, w, start, pad, pin, pout, res, bias_t, bias_s,
    in_sem, own_s, own_r, halo_s, halo_r, p_s, p_r, seed_s, seed_r, seed_h, end_s, end_r, ready,
):
    micro, own, width = out.shape
    heads = width // HEAD
    chunks = heads // GROUP
    half = own // 2
    sections = lax.axis_size("section")
    count = lax.axis_size("seq")
    s = lax.axis_index("section")
    j = lax.axis_index("seq")
    r = lax.axis_index("rep")
    other = 1 - r
    following = lax.rem(s + 1, sections)
    before = jnp.maximum(s - 1, 0)
    first = s == 0
    last = s == sections - 1

    late = first & (j == 0) & (r == 0)
    helper = first & (j == 1) & (r == 0)
    donor = (s == 1) & (j == 0) & (r == 0)
    active = jnp.logical_not(late)

    def number(flag):
        return flag.astype(jnp.int32)

    def sides(to_left, to_right, tile=0):
        at = j - tile

        @pl.when(at > 0)
        def _():
            to_left()

        @pl.when(at < count - 1)
        def _():
            to_right()

    w_copy = pltpu.make_async_copy(w_hbm, w, in_sem.at[0])
    sig_copy = pltpu.make_async_copy(sig_hbm, sig, in_sem.at[1])
    start_copy = pltpu.make_async_copy(start_hbm, start, in_sem.at[2])
    pad_copy = pltpu.make_async_copy(pad_hbm, pad, in_sem.at[3])
    sig_copy.start()
    w_copy.start()
    start_copy.start()
    pad_copy.start()

    barrier = pltpu.get_barrier_semaphore()

    def signal(device):
        pl.semaphore_signal(barrier, inc=1, device_id=device, device_id_type=MESH)

    def greet(section, place, rep):
        is_late = (section == 0) & (place == 0) & (rep == 0)

        @pl.when(jnp.logical_not(is_late & (s == 1)))
        def _():
            signal((section + number(is_late), place, rep))

    left = jnp.maximum(j - 1, 0)
    right = jnp.minimum(j + 1, count - 1)
    has_left = j > 0
    has_right = j < count - 1

    @pl.when(active)
    def _():
        greet(before, j, other)
        sides(lambda: greet(s, left, r), lambda: greet(s, right, r))
        sides(lambda: greet(before, left, other), lambda: greet(before, right, other))

        @pl.when(jnp.logical_not(first))
        def _():
            greet(before, j, r)
            sides(lambda: greet(before, left, r), lambda: greet(before, right, r))

    @pl.when(helper)
    def _():
        signal((s, left, r))

    def lanes(c):
        return pl.ds(c * GROUP * HEAD, GROUP * HEAD)

    def own_copy(t, m, c):
        return pltpu.make_async_remote_copy(
            src_ref=res.at[t, m, :, lanes(c)],
            dst_ref=hid.at[0, m, pl.ds(0, own), lanes(c)],
            send_sem=own_s.at[t, m, c],
            recv_sem=own_r.at[m, c],
            device_id=(following, j - t, r),
            device_id_type=MESH,
        )

    def halo_copy(m, c, side):
        return pltpu.make_async_remote_copy(
            src_ref=hid.at[0, m, pl.ds(side * half, half), lanes(c)],
            dst_ref=hid.at[0, m, pl.ds(own + (1 - side) * half, half), lanes(c)],
            send_sem=halo_s.at[m, c, side],
            recv_sem=halo_r.at[m, c, side],
            device_id=(s, right if side else left, r),
            device_id_type=MESH,
        )

    def seed_copy(m):
        return pltpu.make_async_remote_copy(
            src_ref=res.at[1, m],
            dst_ref=hid.at[1, m, pl.ds(0, own)],
            send_sem=seed_s.at[m],
            recv_sem=seed_r.at[m],
            device_id=(before, right, r),
            device_id_type=MESH,
        )

    def seed_halo_copy(m, c):
        return pltpu.make_async_remote_copy(
            src_ref=res.at[1, m, pl.ds(half, half), lanes(c)],
            dst_ref=hid.at[0, m, pl.ds(own, half), lanes(c)],
            send_sem=seed_h.at[m, c],
            recv_sem=halo_r.at[m, c, 1],
            device_id=(before, right, r),
            device_id_type=MESH,
        )

    def end_copy(m):
        return pltpu.make_async_remote_copy(
            src_ref=res.at[1, m],
            dst_ref=out.at[m],
            send_sem=end_s.at[m],
            recv_sem=end_r.at[m],
            device_id=(s, left, r),
            device_id_type=MESH,
        )

    def p_copy(k, t, m, section, i, rep):
        at = j - t
        place = (jnp.maximum(at - 1, 0), jnp.minimum(at + 1, count - 1), at)[i]
        to = other if rep else r
        moved = number((section == 0) & (place == 0) & (to == 0))
        return pltpu.make_async_remote_copy(
            src_ref=pout.at[k, t, m],
            dst_ref=pin.at[moved, rep, m, i],
            send_sem=p_s.at[k, t, m, i, rep],
            recv_sem=p_r.at[moved, m, i, rep],
            device_id=(section, place + moved, to),
            device_id_type=MESH,
        )

    def p_arrived(t, m, i, rep):
        pltpu.make_async_remote_copy(
            src_ref=pout.at[0, 0, m],
            dst_ref=pin.at[t, rep, m, i],
            send_sem=p_s.at[0, 0, m, i, rep],
            recv_sem=p_r.at[t, m, i, rep],
            device_id=(s, j, other),
            device_id_type=MESH,
        ).wait_recv()

    lane = lax.broadcasted_iota(jnp.int32, (8, HEAD), 1)

    def folded(p):
        wide = lax.broadcasted_iota(jnp.int32, (16, HEAD), 1)
        low, high = p[:16], p[16:]
        p = jnp.where(wide < 64, low + pltpu.roll(low, 64, 1), high + pltpu.roll(high, 64, 1))
        low, high = p[:8], p[8:]
        return jnp.where(
            (lane & 32) == 0, low + pltpu.roll(low, 96, 1), high + pltpu.roll(high, 32, 1)
        )

    def inverse(*parts):
        total = [
            jnp.sum(jnp.where((lane >> 5) == g, p, 0.0), axis=-1, keepdims=True)
            for p, g in parts
        ]
        total = jnp.concatenate(total, axis=0)
        return jnp.broadcast_to(lax.rsqrt(total / (HEADS * HEAD) + 1e-06), (own, HEAD))

    def forward_halo(m, c):
        @pl.when(jnp.logical_not(helper))
        def _():
            sides(lambda: halo_copy(m, c, 0).start(), lambda: None)

        sides(lambda: None, lambda: halo_copy(m, c, 1).start())

    def each_p(k, t, m, section, act):
        act(p_copy(k, t, m, section, 2, 1))
        sides(
            lambda: act(p_copy(k, t, m, section, 0, 1)),
            lambda: act(p_copy(k, t, m, section, 1, 1)),
            t,
        )

        def to_left():
            if k:
                act(p_copy(k, t, m, section, 0, 0))
            else:
                @pl.when(jnp.logical_not(helper))
                def _():
                    act(p_copy(k, t, m, section, 0, 0))

        sides(to_left, lambda: act(p_copy(k, t, m, section, 1, 0)), t)

    def squares(t, m, rows, heads_of):
        total = None
        for h in heads_of:
            x = hid[t, m, rows, h * HEAD : (h + 1) * HEAD].astype(F32)
            total = x * x if total is None else total + x * x
        return total

    every = range(heads)

    def clear(t, rows, i):
        hid[t, :, rows, :] = jnp.zeros((micro, half, width), BF16)
        pin[t, :, :, i] = jnp.zeros((2, micro, 8, HEAD), F32)

    before_own, after_own = pl.ds(own, half), pl.ds(own + half, half)
    sides_missing = (jnp.logical_not(has_left), jnp.logical_not(has_right))

    @pl.when(sides_missing[0] & active)
    def _():
        clear(0, before_own, 1)

    @pl.when(sides_missing[1])
    def _():
        clear(0, after_own, 0)

    @pl.when(helper)
    def _():
        clear(1, before_own, 1)

    sig_copy.wait()

    def relaid(store):
        for m in range(micro):
            partial = jnp.zeros((own, HEAD), F32)
            for h in every:
                cols = slice(h * HEAD, (h + 1) * HEAD)
                x = sig[m, :, :, cols].astype(F32).reshape(own, HEAD)
                partial = partial + x * x
                store(m, cols, x.astype(BF16))
            pout[0, 0, m] = folded(partial)

    @pl.when(first & active)
    def _():
        def store(m, cols, x):
            hid[0, m, pl.ds(0, own), cols] = x

        relaid(store)

    @pl.when(donor)
    def _():
        def store(m, cols, x):
            res[1, m, :, cols] = x

        relaid(store)

    @pl.when(helper)
    def _():
        for m in range(micro):
            hid[1, m, after_own, :] = hid[0, m, pl.ds(0, half), :]
            pin[1, 0, m, 0] = pout[0, 0, m]

    beside = number(has_left) + number(has_right)
    receivers = beside + jnp.where(last, 0, 2 + 2 * beside) + jnp.where(first, 1 + beside, 0)
    fewer = number(helper) + number(first & (j <= 1) & (r == 1))
    receivers = receivers - fewer + 3 * number(donor)
    pl.semaphore_wait(barrier, jnp.where(late, 1, receivers))

    @pl.when(late)
    def _():
        pl.semaphore_signal(ready, inc=1, device_id=(s, right, r), device_id_type=MESH)

    @pl.when((first & active) | donor)
    def _():
        for m in range(micro):
            each_p(0, 0, m, 0, lambda copy: copy.start())

    @pl.when(first & active)
    def _():
        for m in range(micro):
            for c in range(chunks):
                forward_halo(m, c)

    @pl.when(donor)
    def _():
        for m in range(micro):
            for c in range(chunks):
                seed_halo_copy(m, c).start()
            seed_copy(m).start()

    start_copy.wait()
    pad_copy.wait()

    row = lax.broadcasted_iota(jnp.int32, (2 * own, 4 * own), 0)
    col = lax.broadcasted_iota(jnp.int32, (2 * own, 4 * own), 1) & (own - 1)
    key_time = (row >> 2) - jnp.where(row < own, 0, jnp.where(row < own + half, 12, 4))
    key_station = row & 3
    query_time = col >> 2
    query_station = col & 3
    total_steps = count * (own // 4)
    same_time = key_time == query_time
    same_station = key_station == query_station
    close = jnp.abs(key_time - query_time) <= REACH

    def set_bias(t):
        step = (j - t) * (own // 4) + key_time
        for m in range(micro):
            begin = jnp.zeros_like(row)
            end = jnp.zeros_like(row)
            for z in range(4):
                begin = jnp.where(key_station == z, start[m, z], begin)
                end = jnp.where(key_station == z, total_steps - pad[m, z], end)
            valid = (step >= begin) & (step < end)
            keep = same_station & close & (valid | same_time)
            bias_t[t, m] = jnp.where(keep, 0.0, MASKED)
            keep = same_time & (valid | same_station)
            bias_s[t, m] = jnp.where(keep, 0.0, MASKED)[:own]

    set_bias(0)

    @pl.when(helper)
    def _():
        set_bias(1)

    w_copy.wait()
    scale = math.log2(math.e) / math.sqrt(HEAD)

    def normed(t, m, rows, h, inv):
        x = hid[t, m, rows, h * HEAD : (h + 1) * HEAD]
        return (x.astype(F32) * inv).astype(BF16)

    @pl.when(jnp.logical_not(first))
    def _():
        for c in range(chunks):
            own_copy(0, 0, c).wait_recv()
            forward_halo(0, c)

    near = pl.ds(0, own)
    beyond = pl.ds(own, own)

    def attend(t, m, c, inv_near, inv_beyond, sent):
        queries, keys, values = [], [], []
        blank = jnp.zeros((own, HEAD), BF16)
        for i in range(GROUP):
            h = c * GROUP + i
            x = normed(t, m, near, h, inv_near)
            qkv = jnp.dot(x, w[h], preferred_element_type=F32).astype(BF16)
            x = normed(t, m, beyond, h, inv_beyond)
            kv = jnp.dot(x, w[h, :, HEAD:], preferred_element_type=F32).astype(BF16)
            q = qkv[:, :HEAD]
            queries.append(
                jnp.concatenate([q if i == n else blank for n in range(GROUP)], axis=1)
            )
            k = qkv[:, HEAD : 2 * HEAD]
            keys.append(jnp.concatenate([k, kv[:, :HEAD]], axis=0))
            v = qkv[:, 2 * HEAD :]
            values.append(jnp.concatenate([v, kv[:, HEAD:], v], axis=0))
        scores = lax.dot_general(
            jnp.concatenate(keys, axis=1),
            jnp.concatenate(queries, axis=0),
            (((1,), (1,)), ((), ())),
            preferred_element_type=F32,
        ) * scale
        along = scores + bias_t[t, m]
        along = jnp.exp2(along - jnp.max(along, axis=0, keepdims=True))
        along = along * (1.0 / jnp.sum(along, axis=0, keepdims=True))
        across = scores[:own] + bias_s[t, m]
        across = jnp.exp2(across - jnp.max(across, axis=0, keepdims=True))
        across = across * (1.0 / jnp.sum(across, axis=0, keepdims=True))
        mix = jnp.transpose(jnp.concatenate([along, across], axis=0)).astype(BF16)
        for i in range(GROUP):
            h = c * GROUP + i
            update = jnp.dot(
                mix[i * own : (i + 1) * own], values[i], preferred_element_type=F32
            )
            x = hid[t, m, pl.ds(0, own), h * HEAD : (h + 1) * HEAD].astype(F32)
            y = (x + update).astype(BF16)
            res[t, m, :, h * HEAD : (h + 1) * HEAD] = y
            y = y.astype(F32)
            sent = sent + y * y
        return sent

    tiles = 1 + number(helper)

    @pl.loop(0, jnp.where(late, 0, micro * tiles))
    def _(turn):
        m = turn // tiles
        t = turn % tiles

        @pl.when(t == 1)
        def _():
            seed_copy(m).wait_recv()

        mine = folded(squares(t, m, near, every))
        p_arrived(t, m, 2, 1)
        sides(lambda: p_arrived(t, m, 1, 1), lambda: p_arrived(t, m, 0, 1), t)

        @pl.when(t == 0)
        def _():
            sides(lambda: p_arrived(0, m, 1, 0), lambda: p_arrived(0, m, 0, 0))

        mine = mine + pin[t, 1, m, 2]
        inv_near = inverse((mine, 0), (mine, 1), (mine, 2), (mine, 3))
        lower = pin[t, 0, m, 1] + pin[t, 1, m, 1]
        upper = pin[t, 0, m, 0] + pin[t, 1, m, 0]
        inv_beyond = inverse((lower, 2), (lower, 3), (upper, 0), (upper, 1))
        sent = jnp.zeros((own, HEAD), F32)
        for block in BLOCKS:
            for c in block:
                @pl.when(jnp.logical_not(first) & (m + 1 < micro))
                def _():
                    own_copy(0, m + 1, c).wait_recv()
                    forward_halo(m + 1, c)

            @pl.when(t == 0)
            def _():
                sides(
                    lambda: [halo_copy(m, c, 1).wait_recv() for c in block],
                    lambda: [halo_copy(m, c, 0).wait_recv() for c in block],
                )

            for c in block:
                sent = attend(t, m, c, inv_near, inv_beyond, sent)

            @pl.when(jnp.logical_not(last))
            def _():
                for c in block:
                    own_copy(t, m, c).start()

        @pl.when(jnp.logical_not(last))
        def _():
            pout[1, t, m] = folded(sent)
            each_p(1, t, m, following, lambda copy: copy.start())

    @pl.when(active)
    def _():
        out[...] = res[0]

        @pl.when(jnp.logical_not(helper))
        def _():
            sides(
                lambda: [halo_copy(m, c, 0).wait_send() for m in range(micro) for c in range(chunks)],
                lambda: None,
            )

        sides(
            lambda: None,
            lambda: [halo_copy(m, c, 1).wait_send() for m in range(micro) for c in range(chunks)],
        )

    def wait_sent(t):
        for m in range(micro):
            for c in range(chunks):
                own_copy(t, m, c).wait_send()
            each_p(1, t, m, following, lambda copy: copy.wait_send())

    @pl.when(active & jnp.logical_not(last))
    def _():
        wait_sent(0)

    @pl.when((first & active) | donor)
    def _():
        for m in range(micro):
            each_p(0, 0, m, 0, lambda copy: copy.wait_send())

    @pl.when(donor)
    def _():
        for m in range(micro):
            for c in range(chunks):
                seed_halo_copy(m, c).wait_send()
            seed_copy(m).wait_send()

    @pl.when(helper)
    def _():
        wait_sent(1)
        pl.semaphore_wait(ready, 1)
        for m in range(micro):
            end_copy(m).start()
        for m in range(micro):
            end_copy(m).wait_send()

    @pl.when(late)
    def _():
        for m in range(micro):
            end_copy(m).wait_recv()


def body(signal, head_proj, record_start, record_pad):
    micro, times, stations, width = signal.shape
    own = times * stations
    heads = width // HEAD
    chunks = heads // GROUP
    dma = pltpu.SemaphoreType.DMA
    vmem = pl.BlockSpec(memory_space=pltpu.VMEM)
    hbm = pl.BlockSpec(memory_space=pltpu.HBM)
    result = pl.pallas_call(
        kernel,
        name="relay",
        out_shape=jax.ShapeDtypeStruct((micro, own, width), BF16),
        in_specs=[hbm] * 4,
        out_specs=vmem,
        scratch_shapes=[
            pltpu.VMEM(signal.shape, BF16),
            pltpu.VMEM((2, micro, 2 * own, width), BF16),
            pltpu.VMEM((heads, HEAD, 3 * HEAD), BF16),
            pltpu.SMEM(record_start.shape, jnp.int32),
            pltpu.SMEM(record_pad.shape, jnp.int32),
            pltpu.VMEM((2, 2, micro, 3, 8, HEAD), F32),
            pltpu.VMEM((2, 2, micro, 8, HEAD), F32),
            pltpu.VMEM((2, micro, own, width), BF16),
            pltpu.VMEM((2, micro, 2 * own, 4 * own), F32),
            pltpu.VMEM((2, micro, own, 4 * own), F32),
            dma((4,)),
            dma((2, micro, chunks)),
            dma((micro, chunks)),
            dma((micro, chunks, 2)),
            dma((micro, chunks, 2)),
            dma((2, 2, micro, 3, 2)),
            dma((2, micro, 3, 2)),
            dma((micro,)),
            dma((micro,)),
            dma((micro, chunks)),
            dma((micro,)),
            dma((micro,)),
            pltpu.SemaphoreType.REGULAR,
        ],
        compiler_params=pltpu.CompilerParams(
            collective_id=0, has_side_effects=True, vmem_limit_bytes=40 * 2**20
        ),
    )(*[pltpu.with_memory_space_constraint(x, pltpu.HBM) for x in (signal, head_proj[0], record_start, record_pad)])
    return result.reshape(1, micro, times, stations, width)


def solution(mesh):
    return jax.shard_map(
        body,
        mesh=mesh,
        in_specs=(P(None, "seq", None, "rep"), P("section", "rep", None, None), P(), P()),
        out_specs=P("section", None, "seq", None, "rep"),
        check_vma=False,
    )
```

```python
import math

import jax
import jax.numpy as jnp
from jax import lax
from jax.experimental import pallas as pl
from jax.experimental.pallas import tpu as pltpu
from jax.sharding import PartitionSpec as P

HEADS = 32
HEAD = 128
REACH = 4
MESH = pl.DeviceIdType.MESH
F32 = jnp.float32
BF16 = jnp.bfloat16
GROUP = 4
MASKED = -1e30


def kernel(
    sig_hbm, w_hbm, start_hbm, pad_hbm, out,
    sig, hid, w, start, pad, qkv, halo_kv, pin, pout, res, bias_t, bias_s,
    in_sem, own_s, own_r, halo_s, halo_r, p_s, p_r, seed_s, seed_r, seed_h, end_s, end_r, ready,
):
    micro, own, width = out.shape
    heads = width // HEAD
    chunks = heads // GROUP
    half = own // 2
    sections = lax.axis_size("section")
    count = lax.axis_size("seq")
    s = lax.axis_index("section")
    j = lax.axis_index("seq")
    r = lax.axis_index("rep")
    other = 1 - r
    following = lax.rem(s + 1, sections)
    before = jnp.maximum(s - 1, 0)
    first = s == 0
    last = s == sections - 1

    late = first & (j == 0) & (r == 0)
    helper = first & (j == 1) & (r == 0)
    donor = (s == 1) & (j == 0) & (r == 0)
    active = jnp.logical_not(late)

    def number(flag):
        return flag.astype(jnp.int32)

    def sides(to_left, to_right, tile=0):
        at = j - tile

        @pl.when(at > 0)
        def _():
            to_left()

        @pl.when(at < count - 1)
        def _():
            to_right()

    w_copy = pltpu.make_async_copy(w_hbm, w, in_sem.at[0])
    sig_copy = pltpu.make_async_copy(sig_hbm, sig, in_sem.at[1])
    start_copy = pltpu.make_async_copy(start_hbm, start, in_sem.at[2])
    pad_copy = pltpu.make_async_copy(pad_hbm, pad, in_sem.at[3])
    sig_copy.start()
    w_copy.start()
    start_copy.start()
    pad_copy.start()

    barrier = pltpu.get_barrier_semaphore()

    def signal(device):
        pl.semaphore_signal(barrier, inc=1, device_id=device, device_id_type=MESH)

    def greet(section, place, rep):
        is_late = (section == 0) & (place == 0) & (rep == 0)

        @pl.when(jnp.logical_not(is_late & (s == 1)))
        def _():
            signal((section + number(is_late), place, rep))

    left = jnp.maximum(j - 1, 0)
    right = jnp.minimum(j + 1, count - 1)
    has_left = j > 0
    has_right = j < count - 1

    @pl.when(active)
    def _():
        greet(before, j, other)
        sides(lambda: greet(s, left, r), lambda: greet(s, right, r))
        sides(lambda: greet(before, left, other), lambda: greet(before, right, other))

        @pl.when(jnp.logical_not(first))
        def _():
            greet(before, j, r)
            sides(lambda: greet(before, left, r), lambda: greet(before, right, r))

    @pl.when(helper)
    def _():
        signal((s, left, r))

    def lanes(c):
        return pl.ds(c * GROUP * HEAD, GROUP * HEAD)

    def own_copy(t, m, c):
        return pltpu.make_async_remote_copy(
            src_ref=res.at[t, m, :, lanes(c)],
            dst_ref=hid.at[0, m, pl.ds(0, own), lanes(c)],
            send_sem=own_s.at[t, m, c],
            recv_sem=own_r.at[m, c],
            device_id=(following, j - t, r),
            device_id_type=MESH,
        )

    def halo_copy(m, c, side):
        return pltpu.make_async_remote_copy(
            src_ref=hid.at[0, m, pl.ds(side * half, half), lanes(c)],
            dst_ref=hid.at[0, m, pl.ds(own + (1 - side) * half, half), lanes(c)],
            send_sem=halo_s.at[m, c, side],
            recv_sem=halo_r.at[m, c, side],
            device_id=(s, right if side else left, r),
            device_id_type=MESH,
        )

    def seed_copy(m):
        return pltpu.make_async_remote_copy(
            src_ref=res.at[1, m],
            dst_ref=hid.at[1, m, pl.ds(0, own)],
            send_sem=seed_s.at[m],
            recv_sem=seed_r.at[m],
            device_id=(before, right, r),
            device_id_type=MESH,
        )

    def seed_halo_copy(m, c):
        return pltpu.make_async_remote_copy(
            src_ref=res.at[1, m, pl.ds(half, half), lanes(c)],
            dst_ref=hid.at[0, m, pl.ds(own, half), lanes(c)],
            send_sem=seed_h.at[m, c],
            recv_sem=halo_r.at[m, c, 1],
            device_id=(before, right, r),
            device_id_type=MESH,
        )

    def end_copy(m):
        return pltpu.make_async_remote_copy(
            src_ref=res.at[1, m],
            dst_ref=out.at[m],
            send_sem=end_s.at[m],
            recv_sem=end_r.at[m],
            device_id=(s, left, r),
            device_id_type=MESH,
        )

    def p_copy(k, t, m, section, i, rep):
        at = j - t
        place = (jnp.maximum(at - 1, 0), jnp.minimum(at + 1, count - 1), at)[i]
        to = other if rep else r
        moved = number((section == 0) & (place == 0) & (to == 0))
        return pltpu.make_async_remote_copy(
            src_ref=pout.at[k, t, m],
            dst_ref=pin.at[moved, rep, m, i],
            send_sem=p_s.at[k, t, m, i, rep],
            recv_sem=p_r.at[moved, m, i, rep],
            device_id=(section, place + moved, to),
            device_id_type=MESH,
        )

    def p_arrived(t, m, i, rep):
        pltpu.make_async_remote_copy(
            src_ref=pout.at[0, 0, m],
            dst_ref=pin.at[t, rep, m, i],
            send_sem=p_s.at[0, 0, m, i, rep],
            recv_sem=p_r.at[t, m, i, rep],
            device_id=(s, j, other),
            device_id_type=MESH,
        ).wait_recv()

    lane = lax.broadcasted_iota(jnp.int32, (8, HEAD), 1)

    def folded(p):
        wide = lax.broadcasted_iota(jnp.int32, (16, HEAD), 1)
        low, high = p[:16], p[16:]
        p = jnp.where(wide < 64, low + pltpu.roll(low, 64, 1), high + pltpu.roll(high, 64, 1))
        low, high = p[:8], p[8:]
        return jnp.where(
            (lane & 32) == 0, low + pltpu.roll(low, 96, 1), high + pltpu.roll(high, 32, 1)
        )

    def inverse(*parts):
        total = [
            jnp.sum(jnp.where((lane >> 5) == g, p, 0.0), axis=-1, keepdims=True)
            for p, g in parts
        ]
        total = jnp.concatenate(total, axis=0)
        return jnp.broadcast_to(lax.rsqrt(total / (HEADS * HEAD) + 1e-06), (own, HEAD))

    def forward_halo(m, c):
        @pl.when(jnp.logical_not(helper))
        def _():
            sides(lambda: halo_copy(m, c, 0).start(), lambda: None)

        sides(lambda: None, lambda: halo_copy(m, c, 1).start())

    def each_p(k, t, m, section, act):
        act(p_copy(k, t, m, section, 2, 1))
        sides(
            lambda: act(p_copy(k, t, m, section, 0, 1)),
            lambda: act(p_copy(k, t, m, section, 1, 1)),
            t,
        )

        def to_left():
            if k:
                act(p_copy(k, t, m, section, 0, 0))
            else:
                @pl.when(jnp.logical_not(helper))
                def _():
                    act(p_copy(k, t, m, section, 0, 0))

        sides(to_left, lambda: act(p_copy(k, t, m, section, 1, 0)), t)

    def squares(t, m, rows, heads_of):
        total = None
        for h in heads_of:
            x = hid[t, m, rows, h * HEAD : (h + 1) * HEAD].astype(F32)
            total = x * x if total is None else total + x * x
        return total

    every = range(heads)

    def clear(t, rows, i):
        hid[t, :, rows, :] = jnp.zeros((micro, half, width), BF16)
        pin[t, :, :, i] = jnp.zeros((2, micro, 8, HEAD), F32)

    before_own, after_own = pl.ds(own, half), pl.ds(own + half, half)
    sides_missing = (jnp.logical_not(has_left), jnp.logical_not(has_right))

    @pl.when(sides_missing[0] & active)
    def _():
        clear(0, before_own, 1)

    @pl.when(sides_missing[1])
    def _():
        clear(0, after_own, 0)

    @pl.when(helper)
    def _():
        clear(1, before_own, 1)

    sig_copy.wait()

    def relaid(store):
        for m in range(micro):
            partial = jnp.zeros((own, HEAD), F32)
            for h in every:
                cols = slice(h * HEAD, (h + 1) * HEAD)
                x = sig[m, :, :, cols].astype(F32).reshape(own, HEAD)
                partial = partial + x * x
                store(m, cols, x.astype(BF16))
            pout[0, 0, m] = folded(partial)

    @pl.when(first & active)
    def _():
        def store(m, cols, x):
            hid[0, m, pl.ds(0, own), cols] = x

        relaid(store)

    @pl.when(donor)
    def _():
        def store(m, cols, x):
            res[1, m, :, cols] = x

        relaid(store)

    @pl.when(helper)
    def _():
        for m in range(micro):
            hid[1, m, after_own, :] = hid[0, m, pl.ds(0, half), :]
            pin[1, 0, m, 0] = pout[0, 0, m]

    beside = number(has_left) + number(has_right)
    receivers = beside + jnp.where(last, 0, 2 + 2 * beside) + jnp.where(first, 1 + beside, 0)
    fewer = number(helper) + number(first & (j <= 1) & (r == 1))
    receivers = receivers - fewer + 3 * number(donor)
    pl.semaphore_wait(barrier, jnp.where(late, 1, receivers))

    @pl.when(late)
    def _():
        pl.semaphore_signal(ready, inc=1, device_id=(s, right, r), device_id_type=MESH)

    @pl.when((first & active) | donor)
    def _():
        for m in range(micro):
            each_p(0, 0, m, 0, lambda copy: copy.start())

    @pl.when(first & active)
    def _():
        for m in range(micro):
            for c in range(chunks):
                forward_halo(m, c)

    @pl.when(donor)
    def _():
        for m in range(micro):
            for c in range(chunks):
                seed_halo_copy(m, c).start()
            seed_copy(m).start()

    start_copy.wait()
    pad_copy.wait()

    row = lax.broadcasted_iota(jnp.int32, (2 * own, 4 * own), 0)
    col = lax.broadcasted_iota(jnp.int32, (2 * own, 4 * own), 1) & (own - 1)
    key_time = (row >> 2) - jnp.where(row < own, 0, jnp.where(row < own + half, 12, 4))
    key_station = row & 3
    query_time = col >> 2
    query_station = col & 3
    total_steps = count * (own // 4)
    same_time = key_time == query_time
    same_station = key_station == query_station
    close = jnp.abs(key_time - query_time) <= REACH

    def set_bias(t):
        step = (j - t) * (own // 4) + key_time
        for m in range(micro):
            begin = jnp.zeros_like(row)
            end = jnp.zeros_like(row)
            for z in range(4):
                begin = jnp.where(key_station == z, start[m, z], begin)
                end = jnp.where(key_station == z, total_steps - pad[m, z], end)
            valid = (step >= begin) & (step < end)
            keep = same_station & close & (valid | same_time)
            bias_t[t, m] = jnp.where(keep, 0.0, MASKED)
            keep = same_time & (valid | same_station)
            bias_s[t, m] = jnp.where(keep, 0.0, MASKED)[:own]

    set_bias(0)

    @pl.when(helper)
    def _():
        set_bias(1)

    w_copy.wait()
    scale = math.log2(math.e) / math.sqrt(HEAD)

    def normed(t, m, rows, h, inv):
        x = hid[t, m, rows, h * HEAD : (h + 1) * HEAD]
        return (x.astype(F32) * inv).astype(BF16)

    @pl.when(jnp.logical_not(first))
    def _():
        for c in range(chunks):
            own_copy(0, 0, c).wait_recv()
            forward_halo(0, c)

    near = pl.ds(0, own)
    beyond = pl.ds(own, own)

    def project_near(t, m, inv):
        for h in every:
            x = normed(t, m, near, h, inv)
            qkv[h] = jnp.dot(x, w[h], preferred_element_type=F32).astype(BF16)

    def project_beyond(t, m, c, inv):
        for h in range(c * GROUP, (c + 1) * GROUP):
            x = normed(t, m, beyond, h, inv)
            halo_kv[h] = jnp.dot(x, w[h, :, HEAD:], preferred_element_type=F32).astype(BF16)

    def scores_of(c):
        queries, keys = [], []
        blank = jnp.zeros((own, HEAD), BF16)
        for i in range(GROUP):
            h = c * GROUP + i
            q = qkv[h, :, :HEAD]
            queries.append(jnp.concatenate([q if i == n else blank for n in range(GROUP)], axis=1))
            keys.append(jnp.concatenate([qkv[h, :, HEAD : 2 * HEAD], halo_kv[h, :, :HEAD]], axis=0))
        return lax.dot_general(
            jnp.concatenate(keys, axis=1),
            jnp.concatenate(queries, axis=0),
            (((1,), (1,)), ((), ())),
            preferred_element_type=F32,
        ) * scale

    def mixture(t, m, scores):
        along = scores + bias_t[t, m]
        along = jnp.exp2(along - jnp.max(along, axis=0, keepdims=True))
        along = along * (1.0 / jnp.sum(along, axis=0, keepdims=True))
        across = scores[:own] + bias_s[t, m]
        across = jnp.exp2(across - jnp.max(across, axis=0, keepdims=True))
        across = across * (1.0 / jnp.sum(across, axis=0, keepdims=True))
        return jnp.transpose(jnp.concatenate([along, across], axis=0)).astype(BF16)

    def update(t, m, c, mix, sent):
        for i in range(GROUP):
            h = c * GROUP + i
            cols = slice(h * HEAD, (h + 1) * HEAD)
            v = qkv[h, :, 2 * HEAD :]
            values = jnp.concatenate([v, halo_kv[h, :, HEAD:], v], axis=0)
            change = jnp.dot(mix[i * own : (i + 1) * own], values, preferred_element_type=F32)
            y = (hid[t, m, near, cols].astype(F32) + change).astype(BF16)
            res[t, m, :, cols] = y
            y = y.astype(F32)
            sent = sent + y * y
        return sent

    tiles = 1 + number(helper)

    @pl.loop(0, jnp.where(late, 0, micro * tiles))
    def _(turn):
        m = turn // tiles
        t = turn % tiles

        @pl.when(t == 1)
        def _():
            seed_copy(m).wait_recv()

        mine = folded(squares(t, m, near, every))
        p_arrived(t, m, 2, 1)
        mine = mine + pin[t, 1, m, 2]
        project_near(t, m, inverse((mine, 0), (mine, 1), (mine, 2), (mine, 3)))
        sides(lambda: p_arrived(t, m, 1, 1), lambda: p_arrived(t, m, 0, 1), t)

        @pl.when(t == 0)
        def _():
            sides(lambda: p_arrived(0, m, 1, 0), lambda: p_arrived(0, m, 0, 0))

        lower = pin[t, 0, m, 1] + pin[t, 1, m, 1]
        upper = pin[t, 0, m, 0] + pin[t, 1, m, 0]
        inv = inverse((lower, 2), (lower, 3), (upper, 0), (upper, 1))

        def gather(c):
            @pl.when(jnp.logical_not(first) & (m + 1 < micro))
            def _():
                own_copy(0, m + 1, c).wait_recv()
                forward_halo(m + 1, c)

            @pl.when(t == 0)
            def _():
                sides(
                    lambda: halo_copy(m, c, 1).wait_recv(),
                    lambda: halo_copy(m, c, 0).wait_recv(),
                )

        sent = jnp.zeros((own, HEAD), F32)
        gather(0)
        project_beyond(t, m, 0, inv)
        scores = scores_of(0)
        for c in range(chunks):
            later = None
            if c + 1 < chunks:
                gather(c + 1)
                project_beyond(t, m, c + 1, inv)
                later = scores_of(c + 1)
            sent = update(t, m, c, mixture(t, m, scores), sent)
            scores = later

            @pl.when(jnp.logical_not(last))
            def _():
                own_copy(t, m, c).start()

        @pl.when(jnp.logical_not(last))
        def _():
            pout[1, t, m] = folded(sent)
            each_p(1, t, m, following, lambda copy: copy.start())

    @pl.when(active)
    def _():
        out[...] = res[0]

        @pl.when(jnp.logical_not(helper))
        def _():
            sides(
                lambda: [halo_copy(m, c, 0).wait_send() for m in range(micro) for c in range(chunks)],
                lambda: None,
            )

        sides(
            lambda: None,
            lambda: [halo_copy(m, c, 1).wait_send() for m in range(micro) for c in range(chunks)],
        )

    def wait_sent(t):
        for m in range(micro):
            for c in range(chunks):
                own_copy(t, m, c).wait_send()
            each_p(1, t, m, following, lambda copy: copy.wait_send())

    @pl.when(active & jnp.logical_not(last))
    def _():
        wait_sent(0)

    @pl.when((first & active) | donor)
    def _():
        for m in range(micro):
            each_p(0, 0, m, 0, lambda copy: copy.wait_send())

    @pl.when(donor)
    def _():
        for m in range(micro):
            for c in range(chunks):
                seed_halo_copy(m, c).wait_send()
            seed_copy(m).wait_send()

    @pl.when(helper)
    def _():
        wait_sent(1)
        pl.semaphore_wait(ready, 1)
        for m in range(micro):
            end_copy(m).start()
        for m in range(micro):
            end_copy(m).wait_send()

    @pl.when(late)
    def _():
        for m in range(micro):
            end_copy(m).wait_recv()


def body(signal, head_proj, record_start, record_pad):
    micro, times, stations, width = signal.shape
    own = times * stations
    heads = width // HEAD
    chunks = heads // GROUP
    dma = pltpu.SemaphoreType.DMA
    vmem = pl.BlockSpec(memory_space=pltpu.VMEM)
    hbm = pl.BlockSpec(memory_space=pltpu.HBM)
    result = pl.pallas_call(
        kernel,
        name="relay",
        out_shape=jax.ShapeDtypeStruct((micro, own, width), BF16),
        in_specs=[hbm] * 4,
        out_specs=vmem,
        scratch_shapes=[
            pltpu.VMEM(signal.shape, BF16),
            pltpu.VMEM((2, micro, 2 * own, width), BF16),
            pltpu.VMEM((heads, HEAD, 3 * HEAD), BF16),
            pltpu.SMEM(record_start.shape, jnp.int32),
            pltpu.SMEM(record_pad.shape, jnp.int32),
            pltpu.VMEM((heads, own, 3 * HEAD), BF16),
            pltpu.VMEM((heads, own, 2 * HEAD), BF16),
            pltpu.VMEM((2, 2, micro, 3, 8, HEAD), F32),
            pltpu.VMEM((2, 2, micro, 8, HEAD), F32),
            pltpu.VMEM((2, micro, own, width), BF16),
            pltpu.VMEM((2, micro, 2 * own, 4 * own), F32),
            pltpu.VMEM((2, micro, own, 4 * own), F32),
            dma((4,)),
            dma((2, micro, chunks)),
            dma((micro, chunks)),
            dma((micro, chunks, 2)),
            dma((micro, chunks, 2)),
            dma((2, 2, micro, 3, 2)),
            dma((2, micro, 3, 2)),
            dma((micro,)),
            dma((micro,)),
            dma((micro, chunks)),
            dma((micro,)),
            dma((micro,)),
            pltpu.SemaphoreType.REGULAR,
        ],
        compiler_params=pltpu.CompilerParams(
            collective_id=0, has_side_effects=True, vmem_limit_bytes=40 * 2**20
        ),
    )(*[pltpu.with_memory_space_constraint(x, pltpu.HBM) for x in (signal, head_proj[0], record_start, record_pad)])
    return result.reshape(1, micro, times, stations, width)


def solution(mesh):
    return jax.shard_map(
        body,
        mesh=mesh,
        in_specs=(P(None, "seq", None, "rep"), P("section", "rep", None, None), P(), P()),
        out_specs=P("section", None, "seq", None, "rep"),
        check_vma=False,
    )
```

```python
import math

import jax
import jax.numpy as jnp
from jax import lax
from jax.experimental import pallas as pl
from jax.experimental.pallas import tpu as pltpu
from jax.sharding import PartitionSpec as P

HEADS = 32
HEAD = 128
REACH = 4
MESH = pl.DeviceIdType.MESH
F32 = jnp.float32
BF16 = jnp.bfloat16
GROUP = 4
MASKED = -1e30


def kernel(
    sig_hbm, w_hbm, start_hbm, pad_hbm, out,
    sig, hid, w, start, pad, qkv, halo_kv, pin, pout, res, bias_t, bias_s,
    in_sem, own_s, own_r, halo_s, halo_r, p_s, p_r, seed_s, seed_r, seed_h, end_s, end_r, ready,
):
    micro, own, width = out.shape
    heads = width // HEAD
    chunks = heads // GROUP
    half = own // 2
    sections = lax.axis_size("section")
    count = lax.axis_size("seq")
    s = lax.axis_index("section")
    j = lax.axis_index("seq")
    r = lax.axis_index("rep")
    other = 1 - r
    following = lax.rem(s + 1, sections)
    before = jnp.maximum(s - 1, 0)
    first = s == 0
    last = s == sections - 1

    late = first & (j == 0) & (r == 0)
    helper = first & (j == 1) & (r == 0)
    donor = (s == 1) & (j == 0) & (r == 0)
    active = jnp.logical_not(late)

    def number(flag):
        return flag.astype(jnp.int32)

    def sides(to_left, to_right, tile=0):
        at = j - tile

        @pl.when(at > 0)
        def _():
            to_left()

        @pl.when(at < count - 1)
        def _():
            to_right()

    w_copy = pltpu.make_async_copy(w_hbm, w, in_sem.at[0])
    sig_copy = pltpu.make_async_copy(sig_hbm, sig, in_sem.at[1])
    start_copy = pltpu.make_async_copy(start_hbm, start, in_sem.at[2])
    pad_copy = pltpu.make_async_copy(pad_hbm, pad, in_sem.at[3])
    sig_copy.start()
    w_copy.start()
    start_copy.start()
    pad_copy.start()

    barrier = pltpu.get_barrier_semaphore()

    def signal(device):
        pl.semaphore_signal(barrier, inc=1, device_id=device, device_id_type=MESH)

    def greet(section, place, rep):
        is_late = (section == 0) & (place == 0) & (rep == 0)

        @pl.when(jnp.logical_not(is_late & (s == 1)))
        def _():
            signal((section + number(is_late), place, rep))

    left = jnp.maximum(j - 1, 0)
    right = jnp.minimum(j + 1, count - 1)
    has_left = j > 0
    has_right = j < count - 1

    @pl.when(active)
    def _():
        greet(before, j, other)
        sides(lambda: greet(s, left, r), lambda: greet(s, right, r))
        sides(lambda: greet(before, left, other), lambda: greet(before, right, other))

        @pl.when(jnp.logical_not(first))
        def _():
            greet(before, j, r)
            sides(lambda: greet(before, left, r), lambda: greet(before, right, r))

    @pl.when(helper)
    def _():
        signal((s, left, r))

    def lanes(c):
        return pl.ds(c * GROUP * HEAD, GROUP * HEAD)

    def own_copy(t, m, c):
        return pltpu.make_async_remote_copy(
            src_ref=res.at[t, m, :, lanes(c)],
            dst_ref=hid.at[0, m, pl.ds(0, own), lanes(c)],
            send_sem=own_s.at[t, m, c],
            recv_sem=own_r.at[m, c],
            device_id=(following, j - t, r),
            device_id_type=MESH,
        )

    def halo_copy(m, c, side):
        return pltpu.make_async_remote_copy(
            src_ref=hid.at[0, m, pl.ds(side * half, half), lanes(c)],
            dst_ref=hid.at[0, m, pl.ds(own + (1 - side) * half, half), lanes(c)],
            send_sem=halo_s.at[m, c, side],
            recv_sem=halo_r.at[m, c, side],
            device_id=(s, right if side else left, r),
            device_id_type=MESH,
        )

    def seed_copy(m):
        return pltpu.make_async_remote_copy(
            src_ref=res.at[1, m],
            dst_ref=hid.at[1, m, pl.ds(0, own)],
            send_sem=seed_s.at[m],
            recv_sem=seed_r.at[m],
            device_id=(before, right, r),
            device_id_type=MESH,
        )

    def seed_halo_copy(m, c):
        return pltpu.make_async_remote_copy(
            src_ref=res.at[1, m, pl.ds(half, half), lanes(c)],
            dst_ref=hid.at[0, m, pl.ds(own, half), lanes(c)],
            send_sem=seed_h.at[m, c],
            recv_sem=halo_r.at[m, c, 1],
            device_id=(before, right, r),
            device_id_type=MESH,
        )

    def end_copy(m):
        return pltpu.make_async_remote_copy(
            src_ref=res.at[1, m],
            dst_ref=out.at[m],
            send_sem=end_s.at[m],
            recv_sem=end_r.at[m],
            device_id=(s, left, r),
            device_id_type=MESH,
        )

    def p_copy(k, t, m, section, i, rep):
        at = j - t
        place = (jnp.maximum(at - 1, 0), jnp.minimum(at + 1, count - 1), at)[i]
        to = other if rep else r
        moved = number((section == 0) & (place == 0) & (to == 0))
        return pltpu.make_async_remote_copy(
            src_ref=pout.at[k, t, m],
            dst_ref=pin.at[moved, rep, m, i],
            send_sem=p_s.at[k, t, m, i, rep],
            recv_sem=p_r.at[moved, m, i, rep],
            device_id=(section, place + moved, to),
            device_id_type=MESH,
        )

    def p_arrived(t, m, i, rep):
        pltpu.make_async_remote_copy(
            src_ref=pout.at[0, 0, m],
            dst_ref=pin.at[t, rep, m, i],
            send_sem=p_s.at[0, 0, m, i, rep],
            recv_sem=p_r.at[t, m, i, rep],
            device_id=(s, j, other),
            device_id_type=MESH,
        ).wait_recv()

    lane = lax.broadcasted_iota(jnp.int32, (8, HEAD), 1)

    def folded(p):
        wide = lax.broadcasted_iota(jnp.int32, (16, HEAD), 1)
        low, high = p[:16], p[16:]
        p = jnp.where(wide < 64, low + pltpu.roll(low, 64, 1), high + pltpu.roll(high, 64, 1))
        low, high = p[:8], p[8:]
        return jnp.where(
            (lane & 32) == 0, low + pltpu.roll(low, 96, 1), high + pltpu.roll(high, 32, 1)
        )

    def inverse(*parts):
        total = [
            jnp.sum(jnp.where((lane >> 5) == g, p, 0.0), axis=-1, keepdims=True)
            for p, g in parts
        ]
        total = jnp.concatenate(total, axis=0)
        return jnp.broadcast_to(lax.rsqrt(total / (HEADS * HEAD) + 1e-06), (own, HEAD))

    def forward_halo(m, c):
        @pl.when(jnp.logical_not(helper))
        def _():
            sides(lambda: halo_copy(m, c, 0).start(), lambda: None)

        sides(lambda: None, lambda: halo_copy(m, c, 1).start())

    def each_p(k, t, m, section, act):
        act(p_copy(k, t, m, section, 2, 1))
        sides(
            lambda: act(p_copy(k, t, m, section, 0, 1)),
            lambda: act(p_copy(k, t, m, section, 1, 1)),
            t,
        )

        def to_left():
            if k:
                act(p_copy(k, t, m, section, 0, 0))
            else:
                @pl.when(jnp.logical_not(helper))
                def _():
                    act(p_copy(k, t, m, section, 0, 0))

        sides(to_left, lambda: act(p_copy(k, t, m, section, 1, 0)), t)

    def squares(t, m, rows, heads_of):
        total = None
        for h in heads_of:
            x = hid[t, m, rows, h * HEAD : (h + 1) * HEAD].astype(F32)
            total = x * x if total is None else total + x * x
        return total

    every = range(heads)

    def clear(t, rows, i):
        hid[t, :, rows, :] = jnp.zeros((micro, half, width), BF16)
        pin[t, :, :, i] = jnp.zeros((2, micro, 8, HEAD), F32)

    before_own, after_own = pl.ds(own, half), pl.ds(own + half, half)
    sides_missing = (jnp.logical_not(has_left), jnp.logical_not(has_right))

    @pl.when(sides_missing[0] & active)
    def _():
        clear(0, before_own, 1)

    @pl.when(sides_missing[1])
    def _():
        clear(0, after_own, 0)

    @pl.when(helper)
    def _():
        clear(1, before_own, 1)

    sig_copy.wait()

    def relaid(store):
        for m in range(micro):
            partial = jnp.zeros((own, HEAD), F32)
            for h in every:
                cols = slice(h * HEAD, (h + 1) * HEAD)
                x = sig[m, :, :, cols].astype(F32).reshape(own, HEAD)
                partial = partial + x * x
                store(m, cols, x.astype(BF16))
            pout[0, 0, m] = folded(partial)

    @pl.when(first & active)
    def _():
        def store(m, cols, x):
            hid[0, m, pl.ds(0, own), cols] = x

        relaid(store)

    @pl.when(donor)
    def _():
        def store(m, cols, x):
            res[1, m, :, cols] = x

        relaid(store)

    @pl.when(helper)
    def _():
        for m in range(micro):
            hid[1, m, after_own, :] = hid[0, m, pl.ds(0, half), :]
            pin[1, 0, m, 0] = pout[0, 0, m]

    beside = number(has_left) + number(has_right)
    receivers = beside + jnp.where(last, 0, 2 + 2 * beside) + jnp.where(first, 1 + beside, 0)
    fewer = number(helper) + number(first & (j <= 1) & (r == 1))
    receivers = receivers - fewer + 3 * number(donor)
    pl.semaphore_wait(barrier, jnp.where(late, 1, receivers))

    @pl.when(late)
    def _():
        pl.semaphore_signal(ready, inc=1, device_id=(s, right, r), device_id_type=MESH)

    @pl.when((first & active) | donor)
    def _():
        for m in range(micro):
            each_p(0, 0, m, 0, lambda copy: copy.start())

    @pl.when(first & active)
    def _():
        for m in range(micro):
            for c in range(chunks):
                forward_halo(m, c)

    @pl.when(donor)
    def _():
        for m in range(micro):
            for c in range(chunks):
                seed_halo_copy(m, c).start()
            seed_copy(m).start()

    start_copy.wait()
    pad_copy.wait()

    row = lax.broadcasted_iota(jnp.int32, (2 * own, 4 * own), 0)
    col = lax.broadcasted_iota(jnp.int32, (2 * own, 4 * own), 1) & (own - 1)
    key_time = (row >> 2) - jnp.where(row < own, 0, jnp.where(row < own + half, 12, 4))
    key_station = row & 3
    query_time = col >> 2
    query_station = col & 3
    total_steps = count * (own // 4)
    same_time = key_time == query_time
    same_station = key_station == query_station
    close = jnp.abs(key_time - query_time) <= REACH

    def set_bias(t):
        step = (j - t) * (own // 4) + key_time
        for m in range(micro):
            begin = jnp.zeros_like(row)
            end = jnp.zeros_like(row)
            for z in range(4):
                begin = jnp.where(key_station == z, start[m, z], begin)
                end = jnp.where(key_station == z, total_steps - pad[m, z], end)
            valid = (step >= begin) & (step < end)
            keep = same_station & close & (valid | same_time)
            bias_t[t, m] = jnp.where(keep, 0.0, MASKED)
            keep = same_time & (valid | same_station)
            bias_s[t, m] = jnp.where(keep, 0.0, MASKED)[:own]

    set_bias(0)

    @pl.when(helper)
    def _():
        set_bias(1)

    w_copy.wait()
    scale = math.log2(math.e) / math.sqrt(HEAD)

    def normed(t, m, rows, h, inv):
        x = hid[t, m, rows, h * HEAD : (h + 1) * HEAD]
        return (x.astype(F32) * inv).astype(BF16)

    @pl.when(jnp.logical_not(first))
    def _():
        for c in range(chunks):
            own_copy(0, 0, c).wait_recv()
            forward_halo(0, c)

    near = pl.ds(0, own)
    beyond = pl.ds(own, own)

    def project_near(t, m, inv):
        for h in every:
            x = normed(t, m, near, h, inv)
            qkv[h] = jnp.dot(x, w[h], preferred_element_type=F32).astype(BF16)

    def project_beyond(t, m, c, inv):
        for h in range(c * GROUP, (c + 1) * GROUP):
            x = normed(t, m, beyond, h, inv)
            halo_kv[h] = jnp.dot(x, w[h, :, HEAD:], preferred_element_type=F32).astype(BF16)

    def scores_of(c):
        queries, keys = [], []
        blank = jnp.zeros((own, HEAD), BF16)
        for i in range(GROUP):
            h = c * GROUP + i
            q = qkv[h, :, :HEAD]
            queries.append(jnp.concatenate([q if i == n else blank for n in range(GROUP)], axis=1))
            keys.append(jnp.concatenate([qkv[h, :, HEAD : 2 * HEAD], halo_kv[h, :, :HEAD]], axis=0))
        return lax.dot_general(
            jnp.concatenate(keys, axis=1),
            jnp.concatenate(queries, axis=0),
            (((1,), (1,)), ((), ())),
            preferred_element_type=F32,
        ) * scale

    def mixture(t, m, scores):
        along = scores + bias_t[t, m]
        along = jnp.exp2(along - jnp.max(along, axis=0, keepdims=True))
        along = along * (1.0 / jnp.sum(along, axis=0, keepdims=True))
        across = scores[:own] + bias_s[t, m]
        across = jnp.exp2(across - jnp.max(across, axis=0, keepdims=True))
        across = across * (1.0 / jnp.sum(across, axis=0, keepdims=True))
        return jnp.transpose(jnp.concatenate([along, across], axis=0)).astype(BF16)

    def update(t, m, c, mix, sent):
        for i in range(GROUP):
            h = c * GROUP + i
            cols = slice(h * HEAD, (h + 1) * HEAD)
            v = qkv[h, :, 2 * HEAD :]
            values = jnp.concatenate([v, halo_kv[h, :, HEAD:], v], axis=0)
            change = jnp.dot(mix[i * own : (i + 1) * own], values, preferred_element_type=F32)
            y = (hid[t, m, near, cols].astype(F32) + change).astype(BF16)
            res[t, m, :, cols] = y
            y = y.astype(F32)
            sent = sent + y * y
        return sent

    tiles = 1 + number(helper)

    @pl.loop(0, jnp.where(late, 0, micro * tiles))
    def _(turn):
        m = turn // tiles
        t = turn % tiles

        @pl.when(t == 1)
        def _():
            seed_copy(m).wait_recv()

        mine = folded(squares(t, m, near, every))
        p_arrived(t, m, 2, 1)
        mine = mine + pin[t, 1, m, 2]
        project_near(t, m, inverse((mine, 0), (mine, 1), (mine, 2), (mine, 3)))
        sides(lambda: p_arrived(t, m, 1, 1), lambda: p_arrived(t, m, 0, 1), t)

        @pl.when(t == 0)
        def _():
            sides(lambda: p_arrived(0, m, 1, 0), lambda: p_arrived(0, m, 0, 0))

        lower = pin[t, 0, m, 1] + pin[t, 1, m, 1]
        upper = pin[t, 0, m, 0] + pin[t, 1, m, 0]
        inv = inverse((lower, 2), (lower, 3), (upper, 0), (upper, 1))

        def gather(c):
            @pl.when(jnp.logical_not(first) & (m + 1 < micro))
            def _():
                own_copy(0, m + 1, c).wait_recv()
                forward_halo(m + 1, c)

            @pl.when(t == 0)
            def _():
                sides(
                    lambda: halo_copy(m, c, 1).wait_recv(),
                    lambda: halo_copy(m, c, 0).wait_recv(),
                )

        sent = jnp.zeros((own, HEAD), F32)
        gather(0)
        project_beyond(t, m, 0, inv)
        scores = scores_of(0)
        for c in range(chunks):
            later = None
            if c + 1 < chunks:
                gather(c + 1)
                project_beyond(t, m, c + 1, inv)
                later = scores_of(c + 1)
            sent = update(t, m, c, mixture(t, m, scores), sent)
            scores = later

            @pl.when(jnp.logical_not(last))
            def _():
                if c + 1 == chunks:
                    pout[1, t, m] = folded(sent)
                    each_p(1, t, m, following, lambda copy: copy.start())
                own_copy(t, m, c).start()

    @pl.when(active)
    def _():
        out[...] = res[0]

        @pl.when(jnp.logical_not(helper))
        def _():
            sides(
                lambda: [halo_copy(m, c, 0).wait_send() for m in range(micro) for c in range(chunks)],
                lambda: None,
            )

        sides(
            lambda: None,
            lambda: [halo_copy(m, c, 1).wait_send() for m in range(micro) for c in range(chunks)],
        )

    def wait_sent(t):
        for m in range(micro):
            for c in range(chunks):
                own_copy(t, m, c).wait_send()
            each_p(1, t, m, following, lambda copy: copy.wait_send())

    @pl.when(active & jnp.logical_not(last))
    def _():
        wait_sent(0)

    @pl.when((first & active) | donor)
    def _():
        for m in range(micro):
            each_p(0, 0, m, 0, lambda copy: copy.wait_send())

    @pl.when(donor)
    def _():
        for m in range(micro):
            for c in range(chunks):
                seed_halo_copy(m, c).wait_send()
            seed_copy(m).wait_send()

    @pl.when(helper)
    def _():
        wait_sent(1)
        pl.semaphore_wait(ready, 1)
        for m in range(micro):
            end_copy(m).start()
        for m in range(micro):
            end_copy(m).wait_send()

    @pl.when(late)
    def _():
        for m in range(micro):
            end_copy(m).wait_recv()


def body(signal, head_proj, record_start, record_pad):
    micro, times, stations, width = signal.shape
    own = times * stations
    heads = width // HEAD
    chunks = heads // GROUP
    dma = pltpu.SemaphoreType.DMA
    vmem = pl.BlockSpec(memory_space=pltpu.VMEM)
    hbm = pl.BlockSpec(memory_space=pltpu.HBM)
    result = pl.pallas_call(
        kernel,
        name="relay",
        out_shape=jax.ShapeDtypeStruct((micro, own, width), BF16),
        in_specs=[hbm] * 4,
        out_specs=vmem,
        scratch_shapes=[
            pltpu.VMEM(signal.shape, BF16),
            pltpu.VMEM((2, micro, 2 * own, width), BF16),
            pltpu.VMEM((heads, HEAD, 3 * HEAD), BF16),
            pltpu.SMEM(record_start.shape, jnp.int32),
            pltpu.SMEM(record_pad.shape, jnp.int32),
            pltpu.VMEM((heads, own, 3 * HEAD), BF16),
            pltpu.VMEM((heads, own, 2 * HEAD), BF16),
            pltpu.VMEM((2, 2, micro, 3, 8, HEAD), F32),
            pltpu.VMEM((2, 2, micro, 8, HEAD), F32),
            pltpu.VMEM((2, micro, own, width), BF16),
            pltpu.VMEM((2, micro, 2 * own, 4 * own), F32),
            pltpu.VMEM((2, micro, own, 4 * own), F32),
            dma((4,)),
            dma((2, micro, chunks)),
            dma((micro, chunks)),
            dma((micro, chunks, 2)),
            dma((micro, chunks, 2)),
            dma((2, 2, micro, 3, 2)),
            dma((2, micro, 3, 2)),
            dma((micro,)),
            dma((micro,)),
            dma((micro, chunks)),
            dma((micro,)),
            dma((micro,)),
            pltpu.SemaphoreType.REGULAR,
        ],
        compiler_params=pltpu.CompilerParams(
            collective_id=0, has_side_effects=True, vmem_limit_bytes=40 * 2**20
        ),
    )(*[pltpu.with_memory_space_constraint(x, pltpu.HBM) for x in (signal, head_proj[0], record_start, record_pad)])
    return result.reshape(1, micro, times, stations, width)


def solution(mesh):
    return jax.shard_map(
        body,
        mesh=mesh,
        in_specs=(P(None, "seq", None, "rep"), P("section", "rep", None, None), P(), P()),
        out_specs=P("section", None, "seq", None, "rep"),
        check_vma=False,
    )
```

```python
import math

import jax
import jax.numpy as jnp
from jax import lax
from jax.experimental import pallas as pl
from jax.experimental.pallas import tpu as pltpu
from jax.sharding import PartitionSpec as P

HEADS = 32
HEAD = 128
REACH = 4
MESH = pl.DeviceIdType.MESH
F32 = jnp.float32
BF16 = jnp.bfloat16
GROUP = 4
MASKED = -1e30


def kernel(
    sig_hbm, w_hbm, start_hbm, pad_hbm, out,
    sig, hid, w, start, pad, qkv, halo_kv, pin, pout, res, bias_t, bias_s,
    in_sem, own_s, own_r, halo_s, halo_r, p_s, p_r, seed_s, seed_r, seed_h, end_s, end_r, ready,
):
    micro, own, width = out.shape
    heads = width // HEAD
    chunks = heads // GROUP
    half = own // 2
    sections = lax.axis_size("section")
    count = lax.axis_size("seq")
    s = lax.axis_index("section")
    j = lax.axis_index("seq")
    r = lax.axis_index("rep")
    other = 1 - r
    following = lax.rem(s + 1, sections)
    before = jnp.maximum(s - 1, 0)
    first = s == 0
    last = s == sections - 1

    late = first & (j == 0) & (r == 0)
    helper = first & (j == 1) & (r == 0)
    donor = (s == 1) & (j == 0) & (r == 0)
    active = jnp.logical_not(late)

    def number(flag):
        return flag.astype(jnp.int32)

    def sides(to_left, to_right, tile=0):
        at = j - tile

        @pl.when(at > 0)
        def _():
            to_left()

        @pl.when(at < count - 1)
        def _():
            to_right()

    w_copy = pltpu.make_async_copy(w_hbm, w, in_sem.at[0])
    sig_copy = pltpu.make_async_copy(sig_hbm, sig, in_sem.at[1])
    start_copy = pltpu.make_async_copy(start_hbm, start, in_sem.at[2])
    pad_copy = pltpu.make_async_copy(pad_hbm, pad, in_sem.at[3])
    barrier = pltpu.get_barrier_semaphore()

    def signal(device):
        pl.semaphore_signal(barrier, inc=1, device_id=device, device_id_type=MESH)

    def greet(section, place, rep):
        is_late = (section == 0) & (place == 0) & (rep == 0)

        @pl.when(jnp.logical_not(is_late & (s == 1)))
        def _():
            signal((section + number(is_late), place, rep))

    left = jnp.maximum(j - 1, 0)
    right = jnp.minimum(j + 1, count - 1)
    has_left = j > 0
    has_right = j < count - 1

    @pl.when(active)
    def _():
        sides(lambda: greet(before, left, other), lambda: greet(before, right, other))
        greet(before, j, other)
        sides(lambda: greet(s, left, r), lambda: greet(s, right, r))

        @pl.when(jnp.logical_not(first))
        def _():
            greet(before, j, r)
            sides(lambda: greet(before, left, r), lambda: greet(before, right, r))

    @pl.when(helper)
    def _():
        signal((s, left, r))

    sig_copy.start()
    w_copy.start()
    start_copy.start()
    pad_copy.start()

    def lanes(c):
        return pl.ds(c * GROUP * HEAD, GROUP * HEAD)

    def own_copy(t, m, c):
        return pltpu.make_async_remote_copy(
            src_ref=res.at[t, m, :, lanes(c)],
            dst_ref=hid.at[0, m, pl.ds(0, own), lanes(c)],
            send_sem=own_s.at[t, m, c],
            recv_sem=own_r.at[m, c],
            device_id=(following, j - t, r),
            device_id_type=MESH,
        )

    def halo_copy(m, c, side):
        return pltpu.make_async_remote_copy(
            src_ref=hid.at[0, m, pl.ds(side * half, half), lanes(c)],
            dst_ref=hid.at[0, m, pl.ds(own + (1 - side) * half, half), lanes(c)],
            send_sem=halo_s.at[m, c, side],
            recv_sem=halo_r.at[m, c, side],
            device_id=(s, right if side else left, r),
            device_id_type=MESH,
        )

    def seed_copy(m):
        return pltpu.make_async_remote_copy(
            src_ref=res.at[1, m],
            dst_ref=hid.at[1, m, pl.ds(0, own)],
            send_sem=seed_s.at[m],
            recv_sem=seed_r.at[m],
            device_id=(before, right, r),
            device_id_type=MESH,
        )

    def seed_halo_copy(m, c):
        return pltpu.make_async_remote_copy(
            src_ref=res.at[1, m, pl.ds(half, half), lanes(c)],
            dst_ref=hid.at[0, m, pl.ds(own, half), lanes(c)],
            send_sem=seed_h.at[m, c],
            recv_sem=halo_r.at[m, c, 1],
            device_id=(before, right, r),
            device_id_type=MESH,
        )

    def end_copy(m):
        return pltpu.make_async_remote_copy(
            src_ref=res.at[1, m],
            dst_ref=out.at[m],
            send_sem=end_s.at[m],
            recv_sem=end_r.at[m],
            device_id=(s, left, r),
            device_id_type=MESH,
        )

    def p_copy(k, t, m, section, i, rep):
        at = j - t
        place = (jnp.maximum(at - 1, 0), jnp.minimum(at + 1, count - 1), at)[i]
        to = other if rep else r
        moved = number((section == 0) & (place == 0) & (to == 0))
        return pltpu.make_async_remote_copy(
            src_ref=pout.at[k, t, m],
            dst_ref=pin.at[moved, rep, m, i],
            send_sem=p_s.at[k, t, m, i, rep],
            recv_sem=p_r.at[moved, m, i, rep],
            device_id=(section, place + moved, to),
            device_id_type=MESH,
        )

    def p_arrived(t, m, i, rep):
        pltpu.make_async_remote_copy(
            src_ref=pout.at[0, 0, m],
            dst_ref=pin.at[t, rep, m, i],
            send_sem=p_s.at[0, 0, m, i, rep],
            recv_sem=p_r.at[t, m, i, rep],
            device_id=(s, j, other),
            device_id_type=MESH,
        ).wait_recv()

    lane = lax.broadcasted_iota(jnp.int32, (8, HEAD), 1)

    def folded(p):
        wide = lax.broadcasted_iota(jnp.int32, (16, HEAD), 1)
        low, high = p[:16], p[16:]
        p = jnp.where(wide < 64, low + pltpu.roll(low, 64, 1), high + pltpu.roll(high, 64, 1))
        low, high = p[:8], p[8:]
        return jnp.where(
            (lane & 32) == 0, low + pltpu.roll(low, 96, 1), high + pltpu.roll(high, 32, 1)
        )

    def inverse(*parts):
        total = [
            jnp.sum(jnp.where((lane >> 5) == g, p, 0.0), axis=-1, keepdims=True)
            for p, g in parts
        ]
        total = jnp.concatenate(total, axis=0)
        return jnp.broadcast_to(lax.rsqrt(total / (HEADS * HEAD) + 1e-06), (own, HEAD))

    def forward_halo(m, c):
        @pl.when(jnp.logical_not(helper))
        def _():
            sides(lambda: halo_copy(m, c, 0).start(), lambda: None)

        sides(lambda: None, lambda: halo_copy(m, c, 1).start())

    def each_p(k, t, m, section, act):
        act(p_copy(k, t, m, section, 2, 1))
        sides(
            lambda: act(p_copy(k, t, m, section, 0, 1)),
            lambda: act(p_copy(k, t, m, section, 1, 1)),
            t,
        )

        def to_left():
            if k:
                act(p_copy(k, t, m, section, 0, 0))
            else:
                @pl.when(jnp.logical_not(helper))
                def _():
                    act(p_copy(k, t, m, section, 0, 0))

        sides(to_left, lambda: act(p_copy(k, t, m, section, 1, 0)), t)

    def squares(t, m, rows, heads_of):
        total = None
        for h in heads_of:
            x = hid[t, m, rows, h * HEAD : (h + 1) * HEAD].astype(F32)
            total = x * x if total is None else total + x * x
        return total

    every = range(heads)

    def clear(t, rows, i):
        hid[t, :, rows, :] = jnp.zeros((micro, half, width), BF16)
        pin[t, :, :, i] = jnp.zeros((2, micro, 8, HEAD), F32)

    before_own, after_own = pl.ds(own, half), pl.ds(own + half, half)
    sides_missing = (jnp.logical_not(has_left), jnp.logical_not(has_right))

    @pl.when(sides_missing[0] & active)
    def _():
        clear(0, before_own, 1)

    @pl.when(sides_missing[1])
    def _():
        clear(0, after_own, 0)

    @pl.when(helper)
    def _():
        clear(1, before_own, 1)

    sig_copy.wait()

    def relaid(store):
        for m in range(micro):
            partial = jnp.zeros((own, HEAD), F32)
            for h in every:
                cols = slice(h * HEAD, (h + 1) * HEAD)
                x = sig[m, :, :, cols].astype(F32).reshape(own, HEAD)
                partial = partial + x * x
                store(m, cols, x.astype(BF16))
            pout[0, 0, m] = folded(partial)

    @pl.when(first & active)
    def _():
        def store(m, cols, x):
            hid[0, m, pl.ds(0, own), cols] = x

        relaid(store)

    @pl.when(donor)
    def _():
        def store(m, cols, x):
            res[1, m, :, cols] = x

        relaid(store)

    @pl.when(helper)
    def _():
        for m in range(micro):
            hid[1, m, after_own, :] = hid[0, m, pl.ds(0, half), :]
            pin[1, 0, m, 0] = pout[0, 0, m]

    beside = number(has_left) + number(has_right)
    receivers = beside + jnp.where(last, 0, 2 + 2 * beside) + jnp.where(first, 1 + beside, 0)
    fewer = number(helper) + number(first & (j <= 1) & (r == 1))
    receivers = receivers - fewer + 3 * number(donor)
    pl.semaphore_wait(barrier, jnp.where(late, 1, receivers))

    @pl.when(late)
    def _():
        pl.semaphore_signal(ready, inc=1, device_id=(s, right, r), device_id_type=MESH)

    @pl.when((first & active) | donor)
    def _():
        for m in range(micro):
            each_p(0, 0, m, 0, lambda copy: copy.start())

    @pl.when(first & active)
    def _():
        for m in range(micro):
            for c in range(chunks):
                forward_halo(m, c)

    @pl.when(donor)
    def _():
        for m in range(micro):
            for c in range(chunks):
                seed_halo_copy(m, c).start()
            seed_copy(m).start()

    start_copy.wait()
    pad_copy.wait()

    row = lax.broadcasted_iota(jnp.int32, (2 * own, 4 * own), 0)
    col = lax.broadcasted_iota(jnp.int32, (2 * own, 4 * own), 1) & (own - 1)
    key_time = (row >> 2) - jnp.where(row < own, 0, jnp.where(row < own + half, 12, 4))
    key_station = row & 3
    query_time = col >> 2
    query_station = col & 3
    total_steps = count * (own // 4)
    same_time = key_time == query_time
    same_station = key_station == query_station
    close = jnp.abs(key_time - query_time) <= REACH

    def set_bias(t):
        step = (j - t) * (own // 4) + key_time
        for m in range(micro):
            begin = jnp.zeros_like(row)
            end = jnp.zeros_like(row)
            for z in range(4):
                begin = jnp.where(key_station == z, start[m, z], begin)
                end = jnp.where(key_station == z, total_steps - pad[m, z], end)
            valid = (step >= begin) & (step < end)
            keep = same_station & close & (valid | same_time)
            bias_t[t, m] = jnp.where(keep, 0.0, MASKED)
            keep = same_time & (valid | same_station)
            bias_s[t, m] = jnp.where(keep, 0.0, MASKED)[:own]

    set_bias(0)

    @pl.when(helper)
    def _():
        set_bias(1)

    w_copy.wait()
    scale = math.log2(math.e) / math.sqrt(HEAD)

    def normed(t, m, rows, h, inv):
        x = hid[t, m, rows, h * HEAD : (h + 1) * HEAD]
        return (x.astype(F32) * inv).astype(BF16)

    @pl.when(jnp.logical_not(first))
    def _():
        for c in range(chunks):
            own_copy(0, 0, c).wait_recv()
            forward_halo(0, c)

    near = pl.ds(0, own)
    beyond = pl.ds(own, own)

    def project_near(t, m, inv):
        for h in every:
            x = normed(t, m, near, h, inv)
            qkv[h] = jnp.dot(x, w[h], preferred_element_type=F32).astype(BF16)

    def project_beyond(t, m, c, inv):
        for h in range(c * GROUP, (c + 1) * GROUP):
            x = normed(t, m, beyond, h, inv)
            halo_kv[h] = jnp.dot(x, w[h, :, HEAD:], preferred_element_type=F32).astype(BF16)

    def scores_of(c):
        queries, keys = [], []
        blank = jnp.zeros((own, HEAD), BF16)
        for i in range(GROUP):
            h = c * GROUP + i
            q = qkv[h, :, :HEAD]
            queries.append(jnp.concatenate([q if i == n else blank for n in range(GROUP)], axis=1))
            keys.append(jnp.concatenate([qkv[h, :, HEAD : 2 * HEAD], halo_kv[h, :, :HEAD]], axis=0))
        return lax.dot_general(
            jnp.concatenate(keys, axis=1),
            jnp.concatenate(queries, axis=0),
            (((1,), (1,)), ((), ())),
            preferred_element_type=F32,
        ) * scale

    def mixture(t, m, scores):
        along = scores + bias_t[t, m]
        along = jnp.exp2(along - jnp.max(along, axis=0, keepdims=True))
        along = along * (1.0 / jnp.sum(along, axis=0, keepdims=True))
        across = scores[:own] + bias_s[t, m]
        across = jnp.exp2(across - jnp.max(across, axis=0, keepdims=True))
        across = across * (1.0 / jnp.sum(across, axis=0, keepdims=True))
        return jnp.transpose(jnp.concatenate([along, across], axis=0)).astype(BF16)

    def update(t, m, c, mix, sent):
        for i in range(GROUP):
            h = c * GROUP + i
            cols = slice(h * HEAD, (h + 1) * HEAD)
            v = qkv[h, :, 2 * HEAD :]
            values = jnp.concatenate([v, halo_kv[h, :, HEAD:], v], axis=0)
            change = jnp.dot(mix[i * own : (i + 1) * own], values, preferred_element_type=F32)
            y = (hid[t, m, near, cols].astype(F32) + change).astype(BF16)
            res[t, m, :, cols] = y
            y = y.astype(F32)
            sent = sent + y * y
        return sent

    tiles = 1 + number(helper)

    @pl.loop(0, jnp.where(late, 0, micro * tiles))
    def _(turn):
        m = turn // tiles
        t = turn % tiles

        @pl.when(t == 1)
        def _():
            seed_copy(m).wait_recv()

        mine = folded(squares(t, m, near, every))
        p_arrived(t, m, 2, 1)
        mine = mine + pin[t, 1, m, 2]
        project_near(t, m, inverse((mine, 0), (mine, 1), (mine, 2), (mine, 3)))
        sides(lambda: p_arrived(t, m, 1, 1), lambda: p_arrived(t, m, 0, 1), t)

        @pl.when(t == 0)
        def _():
            sides(lambda: p_arrived(0, m, 1, 0), lambda: p_arrived(0, m, 0, 0))

        lower = pin[t, 0, m, 1] + pin[t, 1, m, 1]
        upper = pin[t, 0, m, 0] + pin[t, 1, m, 0]
        inv = inverse((lower, 2), (lower, 3), (upper, 0), (upper, 1))

        def gather(c):
            @pl.when(jnp.logical_not(first) & (m + 1 < micro))
            def _():
                own_copy(0, m + 1, c).wait_recv()
                forward_halo(m + 1, c)

            @pl.when(t == 0)
            def _():
                sides(
                    lambda: halo_copy(m, c, 1).wait_recv(),
                    lambda: halo_copy(m, c, 0).wait_recv(),
                )

        sent = jnp.zeros((own, HEAD), F32)
        gather(0)
        project_beyond(t, m, 0, inv)
        scores = scores_of(0)
        for c in range(chunks):
            later = None
            if c + 1 < chunks:
                gather(c + 1)
                project_beyond(t, m, c + 1, inv)
                later = scores_of(c + 1)
            sent = update(t, m, c, mixture(t, m, scores), sent)
            scores = later

            @pl.when(jnp.logical_not(last))
            def _():
                if c + 1 == chunks:
                    pout[1, t, m] = folded(sent)
                    each_p(1, t, m, following, lambda copy: copy.start())
                own_copy(t, m, c).start()

    @pl.when(active)
    def _():
        out[...] = res[0]

        @pl.when(jnp.logical_not(helper))
        def _():
            sides(
                lambda: [halo_copy(m, c, 0).wait_send() for m in range(micro) for c in range(chunks)],
                lambda: None,
            )

        sides(
            lambda: None,
            lambda: [halo_copy(m, c, 1).wait_send() for m in range(micro) for c in range(chunks)],
        )

    def wait_sent(t):
        for m in range(micro):
            for c in range(chunks):
                own_copy(t, m, c).wait_send()
            each_p(1, t, m, following, lambda copy: copy.wait_send())

    @pl.when(active & jnp.logical_not(last))
    def _():
        wait_sent(0)

    @pl.when((first & active) | donor)
    def _():
        for m in range(micro):
            each_p(0, 0, m, 0, lambda copy: copy.wait_send())

    @pl.when(donor)
    def _():
        for m in range(micro):
            for c in range(chunks):
                seed_halo_copy(m, c).wait_send()
            seed_copy(m).wait_send()

    @pl.when(helper)
    def _():
        wait_sent(1)
        pl.semaphore_wait(ready, 1)
        for m in range(micro):
            end_copy(m).start()
        for m in range(micro):
            end_copy(m).wait_send()

    @pl.when(late)
    def _():
        for m in range(micro):
            end_copy(m).wait_recv()


def body(signal, head_proj, record_start, record_pad):
    micro, times, stations, width = signal.shape
    own = times * stations
    heads = width // HEAD
    chunks = heads // GROUP
    dma = pltpu.SemaphoreType.DMA
    vmem = pl.BlockSpec(memory_space=pltpu.VMEM)
    hbm = pl.BlockSpec(memory_space=pltpu.HBM)
    result = pl.pallas_call(
        kernel,
        name="relay",
        out_shape=jax.ShapeDtypeStruct((micro, own, width), BF16),
        in_specs=[hbm] * 4,
        out_specs=vmem,
        scratch_shapes=[
            pltpu.VMEM(signal.shape, BF16),
            pltpu.VMEM((2, micro, 2 * own, width), BF16),
            pltpu.VMEM((heads, HEAD, 3 * HEAD), BF16),
            pltpu.SMEM(record_start.shape, jnp.int32),
            pltpu.SMEM(record_pad.shape, jnp.int32),
            pltpu.VMEM((heads, own, 3 * HEAD), BF16),
            pltpu.VMEM((heads, own, 2 * HEAD), BF16),
            pltpu.VMEM((2, 2, micro, 3, 8, HEAD), F32),
            pltpu.VMEM((2, 2, micro, 8, HEAD), F32),
            pltpu.VMEM((2, micro, own, width), BF16),
            pltpu.VMEM((2, micro, 2 * own, 4 * own), F32),
            pltpu.VMEM((2, micro, own, 4 * own), F32),
            dma((4,)),
            dma((2, micro, chunks)),
            dma((micro, chunks)),
            dma((micro, chunks, 2)),
            dma((micro, chunks, 2)),
            dma((2, 2, micro, 3, 2)),
            dma((2, micro, 3, 2)),
            dma((micro,)),
            dma((micro,)),
            dma((micro, chunks)),
            dma((micro,)),
            dma((micro,)),
            pltpu.SemaphoreType.REGULAR,
        ],
        compiler_params=pltpu.CompilerParams(
            collective_id=0, has_side_effects=True, vmem_limit_bytes=40 * 2**20
        ),
    )(*[pltpu.with_memory_space_constraint(x, pltpu.HBM) for x in (signal, head_proj[0], record_start, record_pad)])
    return result.reshape(1, micro, times, stations, width)


def solution(mesh):
    return jax.shard_map(
        body,
        mesh=mesh,
        in_specs=(P(None, "seq", None, "rep"), P("section", "rep", None, None), P(), P()),
        out_specs=P("section", None, "seq", None, "rep"),
        check_vma=False,
    )
```

```python
import math

import jax
import jax.numpy as jnp
from jax import lax
from jax.experimental import pallas as pl
from jax.experimental.pallas import tpu as pltpu
from jax.sharding import PartitionSpec as P

HEADS = 32
HEAD = 128
REACH = 4
MESH = pl.DeviceIdType.MESH
F32 = jnp.float32
BF16 = jnp.bfloat16
GROUP = 4
MASKED = -1e30


def kernel(
    sig_hbm, w_hbm, start_hbm, pad_hbm, out,
    sig, hid, w, start, pad, qkv, halo_kv, pin, pout, res, bias_t, bias_s,
    in_sem, own_s, own_r, halo_s, halo_r, p_s, p_r, seed_s, seed_r, seed_h, end_s, end_r, ready,
):
    micro, own, width = out.shape
    heads = width // HEAD
    chunks = heads // GROUP
    half = own // 2
    sections = lax.axis_size("section")
    count = lax.axis_size("seq")
    s = lax.axis_index("section")
    j = lax.axis_index("seq")
    r = lax.axis_index("rep")
    other = 1 - r
    following = lax.rem(s + 1, sections)
    before = jnp.maximum(s - 1, 0)
    first = s == 0
    last = s == sections - 1

    late = first & (j == 0) & (r == 0)
    helper = first & (j == 1) & (r == 0)
    donor = (s == 1) & (j == 0) & (r == 0)
    active = jnp.logical_not(late)

    def number(flag):
        return flag.astype(jnp.int32)

    def sides(to_left, to_right, tile=0):
        at = j - tile

        @pl.when(at > 0)
        def _():
            to_left()

        @pl.when(at < count - 1)
        def _():
            to_right()

    w_copy = pltpu.make_async_copy(w_hbm, w, in_sem.at[0])
    sig_copy = pltpu.make_async_copy(sig_hbm, sig, in_sem.at[1])
    start_copy = pltpu.make_async_copy(start_hbm, start, in_sem.at[2])
    pad_copy = pltpu.make_async_copy(pad_hbm, pad, in_sem.at[3])
    sig_copy.start()
    w_copy.start()
    start_copy.start()
    pad_copy.start()

    barrier = pltpu.get_barrier_semaphore()

    def signal(device):
        pl.semaphore_signal(barrier, inc=1, device_id=device, device_id_type=MESH)

    def greet(section, place, rep):
        is_late = (section == 0) & (place == 0) & (rep == 0)

        @pl.when(jnp.logical_not(is_late & (s == 1)))
        def _():
            signal((section + number(is_late), place, rep))

    left = jnp.maximum(j - 1, 0)
    right = jnp.minimum(j + 1, count - 1)
    has_left = j > 0
    has_right = j < count - 1

    @pl.when(active)
    def _():
        greet(before, j, other)
        sides(lambda: greet(s, left, r), lambda: greet(s, right, r))
        sides(lambda: greet(before, left, other), lambda: greet(before, right, other))

        @pl.when(jnp.logical_not(first))
        def _():
            greet(before, j, r)
            sides(lambda: greet(before, left, r), lambda: greet(before, right, r))

    @pl.when(helper)
    def _():
        signal((s, left, r))

    def lanes(c):
        return pl.ds(c * GROUP * HEAD, GROUP * HEAD)

    def own_copy(t, m, c):
        return pltpu.make_async_remote_copy(
            src_ref=res.at[t, m, :, lanes(c)],
            dst_ref=hid.at[0, m, pl.ds(0, own), lanes(c)],
            send_sem=own_s.at[t, m, c],
            recv_sem=own_r.at[m, c],
            device_id=(following, j - t, r),
            device_id_type=MESH,
        )

    def halo_copy(m, c, side):
        return pltpu.make_async_remote_copy(
            src_ref=hid.at[0, m, pl.ds(side * half, half), lanes(c)],
            dst_ref=hid.at[0, m, pl.ds(own + (1 - side) * half, half), lanes(c)],
            send_sem=halo_s.at[m, c, side],
            recv_sem=halo_r.at[m, c, side],
            device_id=(s, right if side else left, r),
            device_id_type=MESH,
        )

    def seed_copy(m):
        return pltpu.make_async_remote_copy(
            src_ref=res.at[1, m],
            dst_ref=hid.at[1, m, pl.ds(0, own)],
            send_sem=seed_s.at[m],
            recv_sem=seed_r.at[m],
            device_id=(before, right, r),
            device_id_type=MESH,
        )

    def seed_halo_copy(m, c):
        return pltpu.make_async_remote_copy(
            src_ref=res.at[1, m, pl.ds(half, half), lanes(c)],
            dst_ref=hid.at[0, m, pl.ds(own, half), lanes(c)],
            send_sem=seed_h.at[m, c],
            recv_sem=halo_r.at[m, c, 1],
            device_id=(before, right, r),
            device_id_type=MESH,
        )

    def end_copy(m):
        return pltpu.make_async_remote_copy(
            src_ref=res.at[1, m],
            dst_ref=out.at[m],
            send_sem=end_s.at[m],
            recv_sem=end_r.at[m],
            device_id=(s, left, r),
            device_id_type=MESH,
        )

    def p_copy(k, t, m, section, i, rep):
        at = j - t
        place = (jnp.maximum(at - 1, 0), jnp.minimum(at + 1, count - 1), at)[i]
        to = other if rep else r
        moved = number((section == 0) & (place == 0) & (to == 0))
        return pltpu.make_async_remote_copy(
            src_ref=pout.at[k, t, m],
            dst_ref=pin.at[moved, rep, m, i],
            send_sem=p_s.at[k, t, m, i, rep],
            recv_sem=p_r.at[moved, m, i, rep],
            device_id=(section, place + moved, to),
            device_id_type=MESH,
        )

    def p_arrived(t, m, i, rep):
        pltpu.make_async_remote_copy(
            src_ref=pout.at[0, 0, m],
            dst_ref=pin.at[t, rep, m, i],
            send_sem=p_s.at[0, 0, m, i, rep],
            recv_sem=p_r.at[t, m, i, rep],
            device_id=(s, j, other),
            device_id_type=MESH,
        ).wait_recv()

    lane = lax.broadcasted_iota(jnp.int32, (8, HEAD), 1)

    def folded(p):
        wide = lax.broadcasted_iota(jnp.int32, (16, HEAD), 1)
        low, high = p[:16], p[16:]
        p = jnp.where(wide < 64, low + pltpu.roll(low, 64, 1), high + pltpu.roll(high, 64, 1))
        low, high = p[:8], p[8:]
        return jnp.where(
            (lane & 32) == 0, low + pltpu.roll(low, 96, 1), high + pltpu.roll(high, 32, 1)
        )

    def inverse(*parts):
        total = [
            jnp.sum(jnp.where((lane >> 5) == g, p, 0.0), axis=-1, keepdims=True)
            for p, g in parts
        ]
        total = jnp.concatenate(total, axis=0)
        return jnp.broadcast_to(lax.rsqrt(total / (HEADS * HEAD) + 1e-06), (own, HEAD))

    def forward_halo(m, c):
        @pl.when(jnp.logical_not(helper))
        def _():
            sides(lambda: halo_copy(m, c, 0).start(), lambda: None)

        sides(lambda: None, lambda: halo_copy(m, c, 1).start())

    def each_p(k, t, m, section, act):
        act(p_copy(k, t, m, section, 2, 1))
        sides(
            lambda: act(p_copy(k, t, m, section, 0, 1)),
            lambda: act(p_copy(k, t, m, section, 1, 1)),
            t,
        )

        def to_left():
            if k:
                act(p_copy(k, t, m, section, 0, 0))
            else:
                @pl.when(jnp.logical_not(helper))
                def _():
                    act(p_copy(k, t, m, section, 0, 0))

        sides(to_left, lambda: act(p_copy(k, t, m, section, 1, 0)), t)

    def squares(t, m, rows, heads_of):
        total = None
        for h in heads_of:
            x = hid[t, m, rows, h * HEAD : (h + 1) * HEAD].astype(F32)
            total = x * x if total is None else total + x * x
        return total

    every = range(heads)

    def clear(t, rows, i):
        hid[t, :, rows, :] = jnp.zeros((micro, half, width), BF16)
        pin[t, :, :, i] = jnp.zeros((2, micro, 8, HEAD), F32)

    before_own, after_own = pl.ds(own, half), pl.ds(own + half, half)
    sides_missing = (jnp.logical_not(has_left), jnp.logical_not(has_right))

    @pl.when(sides_missing[0] & active)
    def _():
        clear(0, before_own, 1)

    @pl.when(sides_missing[1])
    def _():
        clear(0, after_own, 0)

    @pl.when(helper)
    def _():
        clear(1, before_own, 1)

    sig_copy.wait()

    def relaid(store):
        for m in range(micro):
            partial = jnp.zeros((own, HEAD), F32)
            for h in every:
                cols = slice(h * HEAD, (h + 1) * HEAD)
                x = sig[m, :, :, cols].astype(F32).reshape(own, HEAD)
                partial = partial + x * x
                store(m, cols, x.astype(BF16))
            pout[0, 0, m] = folded(partial)

    @pl.when(first & active)
    def _():
        def store(m, cols, x):
            hid[0, m, pl.ds(0, own), cols] = x

        relaid(store)

    @pl.when(donor)
    def _():
        def store(m, cols, x):
            res[1, m, :, cols] = x

        relaid(store)

    @pl.when(helper)
    def _():
        for m in range(micro):
            hid[1, m, after_own, :] = hid[0, m, pl.ds(0, half), :]
            pin[1, 0, m, 0] = pout[0, 0, m]

    beside = number(has_left) + number(has_right)
    receivers = beside + jnp.where(last, 0, 2 + 2 * beside) + jnp.where(first, 1 + beside, 0)
    fewer = number(helper) + number(first & (j <= 1) & (r == 1))
    receivers = receivers - fewer + 3 * number(donor)
    pl.semaphore_wait(barrier, jnp.where(late, 1, receivers))

    @pl.when(late)
    def _():
        pl.semaphore_signal(ready, inc=1, device_id=(s, right, r), device_id_type=MESH)

    @pl.when((first & active) | donor)
    def _():
        for m in range(micro):
            each_p(0, 0, m, 0, lambda copy: copy.start())

    @pl.when(first & active)
    def _():
        for m in range(micro):
            for c in range(chunks):
                forward_halo(m, c)

    @pl.when(donor)
    def _():
        for m in range(micro):
            for c in range(chunks):
                seed_halo_copy(m, c).start()
            seed_copy(m).start()

    start_copy.wait()
    pad_copy.wait()

    row = lax.broadcasted_iota(jnp.int32, (2 * own, 4 * own), 0)
    col = lax.broadcasted_iota(jnp.int32, (2 * own, 4 * own), 1) & (own - 1)
    key_time = (row >> 2) - jnp.where(row < own, 0, jnp.where(row < own + half, 12, 4))
    key_station = row & 3
    query_time = col >> 2
    query_station = col & 3
    total_steps = count * (own // 4)
    same_time = key_time == query_time
    same_station = key_station == query_station
    close = jnp.abs(key_time - query_time) <= REACH

    def set_bias(t):
        step = (j - t) * (own // 4) + key_time
        for m in range(micro):
            begin = jnp.zeros_like(row)
            end = jnp.zeros_like(row)
            for z in range(4):
                begin = jnp.where(key_station == z, start[m, z], begin)
                end = jnp.where(key_station == z, total_steps - pad[m, z], end)
            valid = (step >= begin) & (step < end)
            keep = same_station & close & (valid | same_time)
            bias_t[t, m] = jnp.where(keep, 0.0, MASKED)
            keep = same_time & (valid | same_station)
            bias_s[t, m] = jnp.where(keep, 0.0, MASKED)[:own]

    set_bias(0)

    @pl.when(helper)
    def _():
        set_bias(1)

    w_copy.wait()
    scale = math.log2(math.e) / math.sqrt(HEAD)

    def normed(t, m, rows, h, inv):
        x = hid[t, m, rows, h * HEAD : (h + 1) * HEAD]
        return (x.astype(F32) * inv).astype(BF16)

    @pl.when(jnp.logical_not(first))
    def _():
        for c in range(chunks):
            own_copy(0, 0, c).wait_recv()
            forward_halo(0, c)

    near = pl.ds(0, own)
    beyond = pl.ds(own, own)

    def project_near(t, m, inv):
        for h in every:
            x = normed(t, m, near, h, inv)
            qkv[h] = jnp.dot(x, w[h], preferred_element_type=F32).astype(BF16)

    def project_beyond(t, m, c, inv):
        for h in range(c * GROUP, (c + 1) * GROUP):
            x = normed(t, m, beyond, h, inv)
            halo_kv[h] = jnp.dot(x, w[h, :, HEAD:], preferred_element_type=F32).astype(BF16)

    def scores_of(c):
        queries, keys = [], []
        blank = jnp.zeros((own, HEAD), BF16)
        for i in range(GROUP):
            h = c * GROUP + i
            q = qkv[h, :, :HEAD]
            queries.append(jnp.concatenate([q if i == n else blank for n in range(GROUP)], axis=1))
            keys.append(jnp.concatenate([qkv[h, :, HEAD : 2 * HEAD], halo_kv[h, :, :HEAD]], axis=0))
        return lax.dot_general(
            jnp.concatenate(keys, axis=1),
            jnp.concatenate(queries, axis=0),
            (((1,), (1,)), ((), ())),
            preferred_element_type=F32,
        ) * scale

    def mixture(t, m, scores):
        along = scores + bias_t[t, m]
        along = jnp.exp2(along - jnp.max(along, axis=0, keepdims=True))
        along = along * (1.0 / jnp.sum(along, axis=0, keepdims=True))
        across = scores[:own] + bias_s[t, m]
        across = jnp.exp2(across - jnp.max(across, axis=0, keepdims=True))
        across = across * (1.0 / jnp.sum(across, axis=0, keepdims=True))
        return jnp.transpose(jnp.concatenate([along, across], axis=0)).astype(BF16)

    def update(t, m, c, mix, sent):
        for i in range(GROUP):
            h = c * GROUP + i
            cols = slice(h * HEAD, (h + 1) * HEAD)
            v = qkv[h, :, 2 * HEAD :]
            values = jnp.concatenate([v, halo_kv[h, :, HEAD:], v], axis=0)
            change = jnp.dot(mix[i * own : (i + 1) * own], values, preferred_element_type=F32)
            y = (hid[t, m, near, cols].astype(F32) + change).astype(BF16)
            res[t, m, :, cols] = y
            y = y.astype(F32)
            sent = sent + y * y
        return sent

    tiles = 1 + number(helper)

    @pl.loop(0, jnp.where(late, 0, micro * tiles))
    def _(turn):
        m = turn // tiles
        t = turn % tiles

        @pl.when(t == 1)
        def _():
            seed_copy(m).wait_recv()

        mine = folded(squares(t, m, near, every))

        @pl.when((t == 0) & (m > 0))
        def _():
            out[m - 1] = res[0, m - 1]

        p_arrived(t, m, 2, 1)
        mine = mine + pin[t, 1, m, 2]
        project_near(t, m, inverse((mine, 0), (mine, 1), (mine, 2), (mine, 3)))
        sides(lambda: p_arrived(t, m, 1, 1), lambda: p_arrived(t, m, 0, 1), t)

        @pl.when(t == 0)
        def _():
            sides(lambda: p_arrived(0, m, 1, 0), lambda: p_arrived(0, m, 0, 0))

        lower = pin[t, 0, m, 1] + pin[t, 1, m, 1]
        upper = pin[t, 0, m, 0] + pin[t, 1, m, 0]
        inv = inverse((lower, 2), (lower, 3), (upper, 0), (upper, 1))

        def gather(c):
            @pl.when(jnp.logical_not(first) & (m + 1 < micro))
            def _():
                own_copy(0, m + 1, c).wait_recv()
                forward_halo(m + 1, c)

            @pl.when(t == 0)
            def _():
                sides(
                    lambda: halo_copy(m, c, 1).wait_recv(),
                    lambda: halo_copy(m, c, 0).wait_recv(),
                )

        sent = jnp.zeros((own, HEAD), F32)
        gather(0)
        project_beyond(t, m, 0, inv)
        scores = scores_of(0)
        for c in range(chunks):
            later = None
            if c + 1 < chunks:
                gather(c + 1)
                project_beyond(t, m, c + 1, inv)
                later = scores_of(c + 1)
            sent = update(t, m, c, mixture(t, m, scores), sent)
            scores = later

            @pl.when(jnp.logical_not(last))
            def _():
                if c + 1 == chunks:
                    pout[1, t, m] = folded(sent)
                    each_p(1, t, m, following, lambda copy: copy.start())
                own_copy(t, m, c).start()

    @pl.when(active)
    def _():
        out[micro - 1] = res[0, micro - 1]

        @pl.when(jnp.logical_not(helper))
        def _():
            sides(
                lambda: [halo_copy(m, c, 0).wait_send() for m in range(micro) for c in range(chunks)],
                lambda: None,
            )

        sides(
            lambda: None,
            lambda: [halo_copy(m, c, 1).wait_send() for m in range(micro) for c in range(chunks)],
        )

    def wait_sent(t):
        for m in range(micro):
            for c in range(chunks):
                own_copy(t, m, c).wait_send()
            each_p(1, t, m, following, lambda copy: copy.wait_send())

    @pl.when(active & jnp.logical_not(last))
    def _():
        wait_sent(0)

    @pl.when((first & active) | donor)
    def _():
        for m in range(micro):
            each_p(0, 0, m, 0, lambda copy: copy.wait_send())

    @pl.when(donor)
    def _():
        for m in range(micro):
            for c in range(chunks):
                seed_halo_copy(m, c).wait_send()
            seed_copy(m).wait_send()

    @pl.when(helper)
    def _():
        wait_sent(1)
        pl.semaphore_wait(ready, 1)
        for m in range(micro):
            end_copy(m).start()
        for m in range(micro):
            end_copy(m).wait_send()

    @pl.when(late)
    def _():
        for m in range(micro):
            end_copy(m).wait_recv()


def body(signal, head_proj, record_start, record_pad):
    micro, times, stations, width = signal.shape
    own = times * stations
    heads = width // HEAD
    chunks = heads // GROUP
    dma = pltpu.SemaphoreType.DMA
    vmem = pl.BlockSpec(memory_space=pltpu.VMEM)
    hbm = pl.BlockSpec(memory_space=pltpu.HBM)
    result = pl.pallas_call(
        kernel,
        name="relay",
        out_shape=jax.ShapeDtypeStruct((micro, own, width), BF16),
        in_specs=[hbm] * 4,
        out_specs=vmem,
        scratch_shapes=[
            pltpu.VMEM(signal.shape, BF16),
            pltpu.VMEM((2, micro, 2 * own, width), BF16),
            pltpu.VMEM((heads, HEAD, 3 * HEAD), BF16),
            pltpu.SMEM(record_start.shape, jnp.int32),
            pltpu.SMEM(record_pad.shape, jnp.int32),
            pltpu.VMEM((heads, own, 3 * HEAD), BF16),
            pltpu.VMEM((heads, own, 2 * HEAD), BF16),
            pltpu.VMEM((2, 2, micro, 3, 8, HEAD), F32),
            pltpu.VMEM((2, 2, micro, 8, HEAD), F32),
            pltpu.VMEM((2, micro, own, width), BF16),
            pltpu.VMEM((2, micro, 2 * own, 4 * own), F32),
            pltpu.VMEM((2, micro, own, 4 * own), F32),
            dma((4,)),
            dma((2, micro, chunks)),
            dma((micro, chunks)),
            dma((micro, chunks, 2)),
            dma((micro, chunks, 2)),
            dma((2, 2, micro, 3, 2)),
            dma((2, micro, 3, 2)),
            dma((micro,)),
            dma((micro,)),
            dma((micro, chunks)),
            dma((micro,)),
            dma((micro,)),
            pltpu.SemaphoreType.REGULAR,
        ],
        compiler_params=pltpu.CompilerParams(
            collective_id=0, has_side_effects=True, vmem_limit_bytes=40 * 2**20
        ),
    )(*[pltpu.with_memory_space_constraint(x, pltpu.HBM) for x in (signal, head_proj[0], record_start, record_pad)])
    return result.reshape(1, micro, times, stations, width)


def solution(mesh):
    return jax.shard_map(
        body,
        mesh=mesh,
        in_specs=(P(None, "seq", None, "rep"), P("section", "rep", None, None), P(), P()),
        out_specs=P("section", None, "seq", None, "rep"),
        check_vma=False,
    )
```
